32 devices in a mesh: dp: 8 (over y, x, core), tensor: 4 (over z).
Axes of the slice: x: 2, y: 2, z: 4, core: 2. Of those that a mesh axis runs over, the one named last changes fastest.
Arguments:
- inputs: bfloat16 [8, 1024, 2048], P('dp', 'tensor'), may hold values from -6 to 6
- teacher: bfloat16 [8, 1024, 2048], P('dp', 'tensor'), may hold values from -6 to 6
- lengths: int32 [8], P('dp'), may hold values from 1 to 1024, 5120 in all
- w_query: bfloat16 [2048, 2048], P('dp', 'tensor'), may hold values from -0.1875 to 0.1875
- w_key: bfloat16 [2048, 2048], P('dp', 'tensor'), may hold values from -0.1875 to 0.1875
- w_value: bfloat16 [2048, 2048], P('dp', 'tensor'), may hold values from -0.125 to 0.125
- w_out: bfloat16 [2048, 2048], P('tensor', 'dp'), may hold values from -2 to 2
- w_gate: bfloat16 [2048, 8192], P('dp', 'tensor'), may hold values from -0.125 to 0.125
- w_up: bfloat16 [2048, 8192], P('dp', 'tensor'), may hold values from -0.125 to 0.125
- w_down: bfloat16 [8192, 2048], P('tensor', 'dp'), may hold values from -0.0625 to 0.0625
Outputs:
- output: bfloat16 [8, 1024, 2048], P('dp', 'tensor')
- loss: float32 [], replicated
- grad_input: float32 [8, 1024, 2048], P('dp', 'tensor')
- grad_query: float32 [2048, 2048], P('dp', 'tensor')
- grad_key: float32 [2048, 2048], P('dp', 'tensor')
- grad_value: float32 [2048, 2048], P('dp', 'tensor')
- grad_out: float32 [2048, 2048], P('tensor', 'dp')
- grad_gate: float32 [2048, 8192], P('dp', 'tensor')
- grad_up: float32 [2048, 8192], P('dp', 'tensor')
- grad_down: float32 [8192, 2048], P('tensor', 'dp')
The draws below stay inside these ranges and needn't reach their ends.
Inputs may be any that keep to these rules, and one draw needn't show every extreme that they name: Sequence s holds lengths[s] valid tokens at its start; its other slots of 1024 are padding; some sequence fills all 1024 slots and the lengths add up to 5120.
All inputs are finite; a program needn't handle non-finite values. No bound on the sum of `lengths` on one device may be relied on, other than what follows from the above.
Results may differ from the reference program's by a relative error of at most 0.015.
The reference program's roundings to bfloat16 on the way count: a program that leaves them out, or rounds other values in their place, can miss the bound.
Values may be sent and summed in bfloat16 or wider, within the bound.
No kernel may reach another device: no remote copies, remote signals or barrier semaphores. Data moves between devices by JAX's collectives and lax.ppermute only.
A program may use at most 192 MiB of HBM per device.

```python
import math
import jax
import jax.numpy as jnp
import numpy as np
from jax import lax

D = 2048
NH = 16
HS = 128
FF = 8192
L = 1024
SEQS = 8
TOKENS = 8192


def block_scale(key, extent, shards, low, high):
    def one(position, blocks):
        steps = jax.random.uniform(jax.random.fold_in(jax.random.fold_in(key, 6), position), (blocks,), jnp.float32, low / len(shards), high / len(shards))
        return jnp.repeat(jnp.exp(steps), extent[position] // blocks).reshape((-1,) + (1,) * (len(extent) - position - 1))

    loudness = one(*shards[0])
    for cut in shards[1:]:
        loudness = loudness * one(*cut)
    return loudness


def length_profile(number_of, total, limit, slope):
    portions = [(1 << 20) // math.isqrt(rank ** slope) + 1 for rank in range(2, number_of + 1)]
    spare, holding = total - limit - (number_of - 1), [1] * (number_of - 1)
    while spare > 0:
        candidates = [i for i in range(number_of - 1) if holding[i] < limit]
        pool, remaining = sum([portions[i] for i in candidates]), spare
        for i in candidates:
            extra = min(limit - holding[i], max(1, remaining * portions[i] // pool), spare)
            holding[i] = holding[i] + extra
            spare = spare - extra
    return np.array([limit] + holding)


def ragged_sizes(stream_key, amount, total, limit, lean):
    if amount == 2:
        one = jax.random.randint(stream_key, (), max(1, total - limit), min(limit, total - 1) + 1)
        return jnp.stack([one, total - one])
    sizes = jnp.asarray(length_profile(amount, total, limit, lean), jnp.int32)
    pairs = (amount - 1) // 2
    source_of, taker = sizes[1:1 + 2 * pairs:2], sizes[2:2 + 2 * pairs:2]
    slack = jnp.minimum(source_of - 1, limit - taker)
    passed = jax.random.randint(jax.random.fold_in(stream_key, 1), (pairs,), 0, 1 << 20) % (slack + 1)
    sizes = sizes.at[1:1 + 2 * pairs:2].set(source_of - passed).at[2:2 + 2 * pairs:2].set(taker + passed)
    return sizes[jax.random.permutation(jax.random.fold_in(stream_key, 2), amount)]


def bell_draw(rng, shape, scale, bound, shards=(), kind=jnp.bfloat16):
    gain = block_scale(rng, shape, shards, -0.22, 0.18) if shards else 1.0
    array = jax.random.normal(rng, shape, jnp.float32) * scale * gain
    return jnp.minimum(jnp.maximum(array, -bound), bound).astype(kind)


def setup_inputs(seed: int = 0) -> dict:
    seeds = jax.random.split(jax.random.key(seed), 11)
    inputs = bell_draw(seeds[0], (SEQS, L, D), 1.0, 6.0, ((0, 8), (1, 4)))
    teacher = bell_draw(seeds[1], (SEQS, L, D), 1.0, 6.0, ((0, 8), (1, 4)))
    lengths = ragged_sizes(seeds[2], SEQS, SEQS * L * 5 // 8, L, 0).astype(jnp.int32)
    w_query = bell_draw(seeds[3], (D, D), (D // 2) ** -0.5, 0.1875, ((0, 8), (1, 4)))
    w_key = bell_draw(seeds[4], (D, D), (D // 2) ** -0.5, 0.1875, ((0, 8), (1, 4)))
    w_value = bell_draw(seeds[5], (D, D), D ** -0.5, 0.125, ((0, 8), (1, 4)))
    w_out = bell_draw(seeds[6], (D, D), (max(D // 256, 2)) ** -0.5, 2.0, ((0, 4), (1, 8)))
    w_gate = bell_draw(seeds[7], (D, FF), D ** -0.5, 0.125, ((0, 8), (1, 4)))
    w_up = bell_draw(seeds[8], (D, FF), D ** -0.5, 0.125, ((0, 8), (1, 4)))
    w_down = bell_draw(seeds[9], (FF, D), FF ** -0.5, 0.0625, ((0, 4), (1, 8)))
    return dict(inputs=inputs, teacher=teacher, lengths=lengths, w_query=w_query, w_key=w_key, w_value=w_value, w_out=w_out, w_gate=w_gate, w_up=w_up, w_down=w_down)


HIGHEST = lax.Precision.HIGHEST
EPSILON = 1e-05

@jax.custom_vjp
def low(v):
    return lax.optimization_barrier(v.astype(jnp.bfloat16)).astype(jnp.float32)

@jax.custom_vjp
def low_back(v):
    return v

def low_keep(v):
    return (low(v), None)

def low_pass(kept, grad):
    return (grad,)

def back_keep(v):
    return (v, None)

def back_low(kept, grad):
    return (low(grad),)
low.defvjp(low_keep, low_pass)
low_back.defvjp(back_keep, back_low)

def layer_norm(values):
    centre = values - lax.optimization_barrier(jnp.mean(values, axis=-1, keepdims=True))
    spread = lax.optimization_barrier(jnp.mean(centre * centre, axis=-1, keepdims=True))
    return centre * lax.rsqrt(spread + EPSILON)

def rotary_tables(length, size):
    half_size = size // 2
    inverse = jnp.exp(jnp.arange(half_size, dtype=jnp.float32) * (-2.0 * math.log(10000.0) / size))
    angles = jnp.arange(length, dtype=jnp.float32)[:, None] * inverse[None, :]
    return (jnp.cos(angles), jnp.sin(angles))

def rotate(values, cosine_table, sine_table):
    half_size = values.shape[-1] // 2
    first_half = values[..., :half_size]
    second_half = values[..., half_size:]
    cosine_rows = cosine_table[:, None, :]
    sine_rows = sine_table[:, None, :]
    return jnp.concatenate([first_half * cosine_rows - second_half * sine_rows, second_half * cosine_rows + first_half * sine_rows], axis=-1)

def one_sequence(seq_in, seq_target, seq_length, w_query, w_key, w_value, w_out, w_gate, w_up, w_down):
    positions = jnp.arange(L)
    cosine_table, sine_table = rotary_tables(L, HS)
    normed = low(layer_norm(seq_in))
    queries = low_back(jnp.dot(normed, w_query, precision=HIGHEST))
    key_raw = low_back(jnp.dot(normed, w_key, precision=HIGHEST))
    values = low(low_back(jnp.dot(normed, w_value, precision=HIGHEST))).reshape(L, NH, HS)
    query_rot = low(rotate(queries.reshape(L, NH, HS), cosine_table, sine_table) * HS ** (-0.5))
    key_rot = low(rotate(key_raw.reshape(L, NH, HS), cosine_table, sine_table))
    scores = low_back(jnp.einsum('qhd,khd->hqk', query_rot, key_rot, precision=HIGHEST))
    causal = positions[:, None] >= positions[None, :]
    scores = jnp.where(causal[None], scores, -1e+30)
    largest = lax.optimization_barrier(jnp.max(scores, axis=-1, keepdims=True))
    shifted = jnp.exp(scores - largest)
    attention = shifted / lax.optimization_barrier(jnp.sum(shifted, axis=-1, keepdims=True))
    mixed_heads = jnp.einsum('hqk,khd->qhd', low(attention), values, precision=HIGHEST).reshape(L, D)
    attended = low(low_back(mixed_heads))
    residual = seq_in + low_back(jnp.dot(attended, w_out, precision=HIGHEST))
    normed_two = low(layer_norm(residual))
    gate_pre = low_back(jnp.dot(normed_two, w_gate, precision=HIGHEST))
    up_pre = low_back(jnp.dot(normed_two, w_up, precision=HIGHEST))
    hidden = low(gate_pre / (1.0 + jnp.exp(-gate_pre)) * up_pre)
    result = residual + low_back(jnp.dot(hidden, w_down, precision=HIGHEST))
    valid_rows = (positions < seq_length)[:, None]
    errors = jnp.where(valid_rows, result - seq_target, 0.0)
    return (result, jnp.sum(errors * errors))

def reference(inputs, teacher, lengths, w_query, w_key, w_value, w_out, w_gate, w_up, w_down):
    float_inputs = inputs.astype(jnp.float32)
    float_target = teacher.astype(jnp.float32)
    float_weights = tuple((matrix.astype(jnp.float32) for matrix in (w_query, w_key, w_value, w_out, w_gate, w_up, w_down)))
    valid_total = jnp.sum(lengths).astype(jnp.float32)
    sequence_step = jax.checkpoint(one_sequence)

    def objective(layer_inputs, *weight_list):

        def scan_body(running, item_pack):
            seq_in, seq_target, seq_length = item_pack
            result, squares = sequence_step(seq_in, seq_target, seq_length, *weight_list)
            return (running + squares, result)
        total_squares, outputs = lax.scan(scan_body, jnp.zeros((), jnp.float32), (layer_inputs, float_target, lengths))
        loss_value = total_squares / (valid_total * D)
        return (loss_value * (TOKENS * D / 2), (outputs, loss_value))
    scaled, pullback, extras = jax.vjp(objective, float_inputs, *float_weights, has_aux=True)
    gradients = pullback(jnp.ones((), jnp.float32))
    outputs, loss_value = extras
    return (outputs.astype(jnp.bfloat16), loss_value, gradients[0], gradients[1], gradients[2], gradients[3], gradients[4], gradients[5], gradients[6], gradients[7])
```

```python
import math

import jax
import jax.numpy as jnp
from jax import lax
from jax.sharding import Mesh
from jax.sharding import PartitionSpec as P

HS = 128
EPSILON = 1e-05
BF = jnp.bfloat16
F32 = jnp.float32


def layer_norm(values):
    centre = values - jnp.mean(values, axis=-1, keepdims=True)
    spread = jnp.mean(centre * centre, axis=-1, keepdims=True)
    return centre * lax.rsqrt(spread + EPSILON)


def norm_back(values, grad_in):
    centre = values - jnp.mean(values, axis=-1, keepdims=True)
    spread = jnp.mean(centre * centre, axis=-1, keepdims=True)
    inverse = lax.rsqrt(spread + EPSILON)
    normed = centre * inverse
    return inverse * (
        grad_in
        - jnp.mean(grad_in, axis=-1, keepdims=True)
        - normed * jnp.mean(grad_in * normed, axis=-1, keepdims=True)
    )


def rotary_tables(length, size):
    half_size = size // 2
    inverse = jnp.exp(jnp.arange(half_size, dtype=F32) * (-2.0 * math.log(10000.0) / size))
    angles = jnp.arange(length, dtype=F32)[:, None] * inverse[None, :]
    return (jnp.cos(angles), jnp.sin(angles))


def rotate(values, cosine_table, sine_table):
    half_size = values.shape[-1] // 2
    first_half = values[..., :half_size]
    second_half = values[..., half_size:]
    cosine_rows = cosine_table[:, None, :]
    sine_rows = sine_table[:, None, :]
    return jnp.concatenate(
        [
            first_half * cosine_rows - second_half * sine_rows,
            second_half * cosine_rows + first_half * sine_rows,
        ],
        axis=-1,
    )


def dot(left, right):
    return jnp.dot(left, right, preferred_element_type=F32)


def dot_nt(left, right):
    return lax.dot_general(left, right, (((1,), (1,)), ((), ())), preferred_element_type=F32)


def dot_tn(left, right):
    return lax.dot_general(left, right, (((0,), (0,)), ((), ())), preferred_element_type=F32)


class PlainLinks:
    line = "tensor"
    rows = "dp"
    everything = ("dp", "tensor")

    def order(self, values):
        return values

    def unorder(self, values):
        return values

    def gather_in(self, shard):
        return lax.all_gather(shard, "dp", axis=0, tiled=True)

    def gather_out(self, shard):
        return lax.all_gather(shard, "dp", axis=1, tiled=True)

    gather_hidden_in = gather_in
    gather_hidden_out = gather_out

    def scatter_in(self, grad):
        return lax.psum_scatter(grad, "dp", scatter_dimension=0, tiled=True).astype(F32)

    def scatter_out(self, grad):
        return lax.psum_scatter(grad, "dp", scatter_dimension=1, tiled=True).astype(F32)

    scatter_hidden_in = scatter_in
    scatter_hidden_out = scatter_out

    def tokens_in(self, values):
        return lax.all_gather(values, "tensor", axis=0, tiled=True)

    def tokens_out(self, partial):
        return lax.psum_scatter(
            partial.astype(BF), "tensor", scatter_dimension=0, tiled=True
        ).astype(F32)


SWAP = [(0, 1), (1, 0)]


def halves(values, axis):
    size = values.shape[axis] // 2
    return (
        lax.slice_in_dim(values, 0, size, axis=axis),
        lax.slice_in_dim(values, size, 2 * size, axis=axis),
    )


def plus(left, right):
    return (left.astype(F32) + right.astype(F32)).astype(BF)


class BlockLinks:
    line = "z"
    rows = ("y", "x", "core")
    everything = ("y", "x", "core", "z")

    def swap(self, values, axis):
        return lax.ppermute(values, axis, SWAP)

    def order(self, values):
        block = values.shape[1] // 8
        y, core = lax.axis_index("y"), lax.axis_index("core")
        parts = []
        for core_slot in range(2):
            for y_slot in range(2):
                for x in range(2):
                    source = (y ^ y_slot) * 4 + x * 2 + (core ^ core_slot)
                    parts.append(lax.dynamic_slice_in_dim(values, source * block, block, axis=1))
        return jnp.concatenate(parts, axis=1)

    def unorder(self, values):
        block = values.shape[1] // 8
        y, core = lax.axis_index("y"), lax.axis_index("core")
        parts = []
        for y_block in range(2):
            for x in range(2):
                for core_block in range(2):
                    slot = (core ^ core_block) * 4 + (y ^ y_block) * 2 + x
                    parts.append(lax.dynamic_slice_in_dim(values, slot * block, block, axis=1))
        return jnp.concatenate(parts, axis=1)

    def by_x(self, own, other, axis):
        first = lax.axis_index("x") == 0
        return jnp.concatenate(
            [jnp.where(first, own, other), jnp.where(first, other, own)], axis=axis
        )

    def of_x(self, values, axis, flip=False):
        size = values.shape[axis] // 2
        place = lax.axis_index("x")
        if flip:
            place = 1 - place
        return lax.dynamic_slice_in_dim(values, place * size, size, axis=axis)

    def join(self, values, received, axis):
        return jnp.concatenate([values, received], axis=axis)

    def gather(self, shard, axis):
        value = self.by_x(shard, self.swap(shard, "x"), axis)
        value = self.join(value, self.swap(value, "y"), axis)
        return self.join(value, self.swap(value, "core"), axis)

    def gather_in(self, shard):
        return self.gather(shard, 0)

    def gather_out(self, shard):
        return self.gather(shard, 1)

    gather_hidden_in = gather_in
    gather_hidden_out = gather_out

    def fold(self, grad, axis, name):
        keep, send = halves(grad, axis)
        return plus(keep, self.swap(send, name))

    def scatter(self, grad, axis):
        grad = self.fold(self.fold(grad, axis, "core"), axis, "y")
        received = self.swap(self.of_x(grad, axis, flip=True), "x")
        return self.of_x(grad, axis).astype(F32) + received.astype(F32)

    def scatter_in(self, grad):
        return self.scatter(grad, 0)

    def scatter_out(self, grad):
        return self.scatter(grad, 1)

    scatter_hidden_in = scatter_in
    scatter_hidden_out = scatter_out

    def tokens_in(self, values):
        return lax.all_gather(values, "z", axis=0, tiled=True)

    def tokens_out(self, partial):
        return lax.psum_scatter(
            partial.astype(BF), "z", scatter_dimension=0, tiled=True
        ).astype(F32)


def layer(links, inputs, teacher, lengths, w_query, w_key, w_value, w_out, w_gate, w_up, w_down):
    line = links.line
    tensor_count = lax.axis_size(line)
    local_rows = inputs.shape[1]
    slot_count = local_rows * tensor_count
    token_total = slot_count * lax.axis_size(links.rows)
    width_all = inputs.shape[2]
    own_length = lengths[0]
    valid_total = lax.psum(own_length.astype(F32), links.rows)
    rows_in = links.order(inputs[0]).astype(F32)
    target = links.order(teacher[0]).astype(F32)
    positions = lax.axis_index(line) * local_rows + jnp.arange(local_rows, dtype=jnp.int32)
    valid_rows = (positions < own_length)[:, None]
    normed = layer_norm(rows_in).astype(BF)
    features = lax.all_gather(normed, line, axis=0, tiled=True)

    head_cols = w_query.shape[1]
    heads_full = links.gather_in(jnp.concatenate([w_query, w_key, w_value], axis=1))
    out_full = links.gather_out(w_out)
    gate_full = links.gather_hidden_in(w_gate)
    up_full = links.gather_hidden_in(w_up)
    down_full = links.gather_hidden_out(w_down)

    head_count = head_cols // HS
    cosine_table, sine_table = rotary_tables(slot_count, HS)
    query_scale = HS ** (-0.5)
    block_rows = min(slot_count, 512)
    block_count = slot_count // block_rows
    key_index = jnp.arange(slot_count, dtype=jnp.int32)
    mixed_in = dot(features, heads_full)
    queries = mixed_in[:, :head_cols]
    key_raw = mixed_in[:, head_cols : 2 * head_cols]
    value_raw = mixed_in[:, 2 * head_cols :]
    query_rot = (
        rotate(queries.reshape(slot_count, head_count, HS), cosine_table, sine_table) * query_scale
    ).astype(BF)
    key_rot = rotate(
        key_raw.reshape(slot_count, head_count, HS), cosine_table, sine_table
    ).astype(BF)
    value_heads = value_raw.reshape(slot_count, head_count, HS).astype(BF)

    def block_scores(block):
        start = block * block_rows
        query_rows = query_rot[start : start + block_rows]
        scores = jnp.einsum("qhd,khd->hqk", query_rows, key_rot, preferred_element_type=F32)
        causal = (start + jnp.arange(block_rows, dtype=jnp.int32))[:, None] >= key_index[None, :]
        return (jnp.where(causal[None], scores, -1e30), query_rows)

    mixed_blocks = []
    lse_blocks = []
    for block in range(block_count):
        scores, query_rows = block_scores(block)
        largest = jnp.max(scores, axis=-1, keepdims=True)
        shifted = jnp.exp(scores - largest)
        totals = jnp.sum(shifted, axis=-1, keepdims=True)
        attention = shifted / totals
        lse_blocks.append(largest + jnp.log(totals))
        mixed_blocks.append(
            jnp.einsum(
                "hqk,khd->qhd", attention.astype(BF), value_heads, preferred_element_type=F32
            )
        )
    attended = jnp.concatenate(mixed_blocks, axis=0).reshape(slot_count, head_cols).astype(BF)
    attn_out = lax.psum_scatter(
        dot(attended, out_full).astype(BF), line, scatter_dimension=0, tiled=True
    ).astype(F32)
    residual = rows_in + attn_out
    normed_two = layer_norm(residual).astype(BF)

    features_two = links.tokens_in(normed_two)
    gate_pre = dot(features_two, gate_full)
    up_pre = dot(features_two, up_full)
    gate_sigmoid = jax.nn.sigmoid(gate_pre)
    activated = gate_pre * gate_sigmoid
    hidden = (activated * up_pre).astype(BF)
    mlp_out = links.tokens_out(dot(hidden, down_full))
    result = residual + mlp_out
    errors = jnp.where(valid_rows, result - target, 0.0)
    squares = jnp.sum(errors * errors)
    total_squares = lax.psum(squares, links.everything)
    loss_value = total_squares / (valid_total * width_all)
    grad_result = errors * (token_total / valid_total)

    down_grad_in = links.tokens_in(grad_result.astype(BF))
    hidden_grad = dot_nt(down_grad_in, down_full)
    gate_grad = (
        hidden_grad * up_pre * gate_sigmoid * (1.0 + gate_pre * (1.0 - gate_sigmoid))
    ).astype(BF)
    up_grad = (hidden_grad * activated).astype(BF)
    feature_grad = dot_nt(gate_grad, gate_full) + dot_nt(up_grad, up_full)
    normed_two_grad = links.tokens_out(feature_grad)
    grad_down = links.scatter_hidden_out(dot_tn(hidden, down_grad_in).astype(BF))
    grad_gate = links.scatter_hidden_in(dot_tn(features_two, gate_grad).astype(BF))
    grad_up = links.scatter_hidden_in(dot_tn(features_two, up_grad).astype(BF))

    residual_grad = grad_result + norm_back(residual, normed_two_grad)
    attn_grad_in = lax.all_gather(residual_grad.astype(BF), line, axis=0, tiled=True)
    grad_out = links.scatter_out(dot_tn(attended, attn_grad_in).astype(BF))
    mixed_grad = dot_nt(attn_grad_in, out_full).astype(BF).reshape(slot_count, head_count, HS)
    value_grad = jnp.zeros((slot_count, head_count, HS), F32)
    key_grad = jnp.zeros((slot_count, head_count, HS), F32)
    query_parts = []
    for block in range(block_count):
        scores, query_rows = block_scores(block)
        attention = jnp.exp(scores - lse_blocks[block])
        start = block * block_rows
        mixed_rows = mixed_grad[start : start + block_rows]
        value_grad = value_grad + jnp.einsum(
            "hqk,qhd->khd", attention.astype(BF), mixed_rows, preferred_element_type=F32
        )
        prob_grad = jnp.einsum("qhd,khd->hqk", mixed_rows, value_heads, preferred_element_type=F32)
        score_grad = (
            attention * (prob_grad - jnp.sum(prob_grad * attention, axis=-1, keepdims=True))
        ).astype(BF)
        query_parts.append(
            jnp.einsum("hqk,khd->qhd", score_grad, key_rot, preferred_element_type=F32)
        )
        key_grad = key_grad + jnp.einsum(
            "hqk,qhd->khd", score_grad, query_rows, preferred_element_type=F32
        )
    query_grad = (
        rotate(jnp.concatenate(query_parts, axis=0), cosine_table, -sine_table) * query_scale
    ).astype(BF)
    key_grad_low = rotate(key_grad, cosine_table, -sine_table).astype(BF)
    heads_grad = jnp.concatenate(
        [
            query_grad.reshape(slot_count, head_cols),
            key_grad_low.reshape(slot_count, head_cols),
            value_grad.astype(BF).reshape(slot_count, head_cols),
        ],
        axis=1,
    )
    normed_grad = lax.psum_scatter(
        dot_nt(heads_grad, heads_full).astype(BF), line, scatter_dimension=0, tiled=True
    ).astype(F32)
    grad_heads = links.scatter_in(dot_tn(features, heads_grad).astype(BF))
    input_grad = residual_grad + norm_back(rows_in, normed_grad)
    return (
        links.unorder(result.astype(BF))[None],
        loss_value,
        links.unorder(input_grad)[None],
        grad_heads[:, :head_cols],
        grad_heads[:, head_cols : 2 * head_cols],
        grad_heads[:, 2 * head_cols :],
        grad_out,
        grad_gate,
        grad_up,
        grad_down,
    )


def solution(mesh):
    if mesh.shape["dp"] == 8 and mesh.shape["tensor"] == 4:
        links = BlockLinks()
        mesh = Mesh(mesh.devices.reshape(2, 2, 2, 4), ("y", "x", "core", "z"))
    else:
        links = PlainLinks()
    dp, tensor = links.rows, links.line
    tokens = P(dp, tensor, None)
    rows = P(dp, tensor)
    cols = P(tensor, dp)
    in_specs = (tokens, tokens, P(dp), rows, rows, rows, cols, rows, rows, cols)
    out_specs = (tokens, P(), tokens, rows, rows, rows, cols, rows, rows, cols)

    def local(*args):
        return layer(links, *args)

    return jax.shard_map(
        local, mesh=mesh, in_specs=in_specs, out_specs=out_specs, check_vma=False
    )
```

```python
import functools
import math

import jax
import jax.numpy as jnp
from jax import lax
from jax.experimental import pallas as pl
from jax.experimental.pallas import tpu as pltpu
from jax.sharding import Mesh
from jax.sharding import PartitionSpec as P

HS = 128
EPSILON = 1e-05
BF = jnp.bfloat16
F32 = jnp.float32
NEGATIVE = -1e30


def statistics(values):
    centre = values - jnp.mean(values, axis=-1, keepdims=True)
    spread = jnp.mean(centre * centre, axis=-1, keepdims=True)
    inverse = lax.rsqrt(spread + EPSILON)
    return centre * inverse, inverse


def norm_back(values, grad_in):
    normed, inverse = statistics(values)
    return inverse * (
        grad_in
        - jnp.mean(grad_in, axis=-1, keepdims=True)
        - normed * jnp.mean(grad_in * normed, axis=-1, keepdims=True)
    )


def rotary_tables(length, size):
    half_size = size // 2
    inverse = jnp.exp(jnp.arange(half_size, dtype=F32) * (-2.0 * math.log(10000.0) / size))
    angles = jnp.arange(length, dtype=F32)[:, None] * inverse[None, :]
    cosine, sine = jnp.cos(angles), jnp.sin(angles)
    return (
        jnp.concatenate([cosine, cosine], axis=1),
        jnp.concatenate([-sine, sine], axis=1),
    )


def dot(left, right):
    return jnp.dot(left, right, preferred_element_type=F32)


def dot_nt(left, right):
    return lax.dot_general(left, right, (((1,), (1,)), ((), ())), preferred_element_type=F32)


def dot_tn(left, right):
    return lax.dot_general(left, right, (((0,), (0,)), ((), ())), preferred_element_type=F32)


def kernel_call(body, grid, ins, outs, args, flops, scratch=(), limit=48):
    args = tuple(
        pltpu.with_memory_space_constraint(a, pltpu.HBM) if a.size > 1024 else a for a in args
    )
    moved = sum(a.size * a.dtype.itemsize for a in args)
    moved += sum(math.prod(shape.shape) * shape.dtype.itemsize for shape, _ in outs)
    return pl.pallas_call(
        body,
        grid=grid,
        in_specs=ins,
        out_specs=[spec for _, spec in outs],
        out_shape=[pltpu.HBM(shape.shape, shape.dtype) for shape, _ in outs],
        scratch_shapes=list(scratch),
        compiler_params=pltpu.CompilerParams(
            dimension_semantics=("arbitrary",) * len(grid), vmem_limit_bytes=limit << 20
        ),
        cost_estimate=pl.CostEstimate(flops=flops, transcendentals=0, bytes_accessed=moved),
    )(*args)


def whole(array):
    rank = len(array.shape)
    return pl.BlockSpec(array.shape, lambda *_: (0,) * rank, pipeline_mode=pl.Buffered(1))


def shape_of(shape, dtype):
    return jax.ShapeDtypeStruct(shape, dtype)


def dot_parts(left, parts, transposed=False):
    total, start = None, 0
    for part in parts:
        depth = part.shape[1 if transposed else 0]
        got = (dot_nt if transposed else dot)(left[:, start : start + depth], part)
        total = got if total is None else total + got
        start += depth
    return total


def heads_body(head_cols, count, x_ref, *refs):
    weights = refs[:count]
    c_ref, s_ref, q_ref, k_ref, v_ref = refs[count:]
    rows = x_ref[...]
    cosine, sine = c_ref[...], s_ref[...]
    for part, out_ref in enumerate((q_ref, k_ref, v_ref)):
        cols = slice(part * head_cols, (part + 1) * head_cols)
        got = dot_parts(rows, [w_ref[:, cols] for w_ref in weights])
        if part == 2:
            out_ref[...] = got.astype(BF)
            continue
        for start in range(0, head_cols, HS):
            head = got[:, start : start + HS]
            turned = head * cosine + pltpu.roll(head, HS // 2, axis=1) * sine
            if part == 0:
                turned = turned * (HS**-0.5)
            out_ref[:, start : start + HS] = turned.astype(BF)


def project_heads(features, weights, tables):
    tokens, width = features.shape
    head_cols = weights[0].shape[1] // 3
    rows = min(256, tokens)
    row_spec = pl.BlockSpec((rows, width), lambda i: (i, 0))
    table_spec = pl.BlockSpec((rows, HS), lambda i: (i, 0))
    out_spec = pl.BlockSpec((rows, head_cols), lambda i: (i, 0))
    out = (shape_of((tokens, head_cols), BF), out_spec)
    return kernel_call(
        functools.partial(heads_body, head_cols, len(weights)),
        (tokens // rows,),
        [row_spec, *map(whole, weights), table_spec, table_spec],
        [out, out, out],
        (features, *weights, *tables),
        2 * tokens * width * 3 * head_cols,
    )


def causal_scores(query, keys, start):
    scores = dot_nt(query, keys)
    row = start + lax.broadcasted_iota(jnp.int32, scores.shape, 0)
    return jnp.where(row >= lax.broadcasted_iota(jnp.int32, scores.shape, 1), scores, NEGATIVE)


def attend_body(rows, q_ref, k_ref, v_ref, o_ref, lse_ref):
    for start in range(0, q_ref.shape[0], rows):
        end = start + rows
        scores = causal_scores(q_ref[start:end, :], k_ref[:end, :], start)
        largest = jnp.max(scores, axis=-1, keepdims=True)
        shifted = jnp.exp(scores - largest)
        total = jnp.sum(shifted, axis=-1, keepdims=True)
        share = (shifted * (1.0 / total)).astype(BF)
        o_ref[start:end, :] = dot(share, v_ref[:end, :]).astype(BF)
        lse_ref[start:end, :] = jnp.broadcast_to(largest + jnp.log(total), (rows, HS))


def attend(query, key, value):
    tokens, head_cols = query.shape
    spec = pl.BlockSpec((tokens, HS), lambda h: (0, h))
    return kernel_call(
        functools.partial(attend_body, min(256, tokens)),
        (head_cols // HS,),
        [spec] * 3,
        [(shape_of((tokens, head_cols), BF), spec), (shape_of((tokens, head_cols), F32), spec)],
        (query, key, value),
        3 * tokens * tokens * head_cols,
    )


def attend_back_body(
    rows, heads, q_ref, k_ref, v_ref, g_ref, lse_ref, c_ref, s_ref, out_ref, dk_ref, dv_ref
):
    tokens = q_ref.shape[0]
    place = pl.program_id(0) * HS
    dk_ref[...] = jnp.zeros_like(dk_ref)
    dv_ref[...] = jnp.zeros_like(dv_ref)

    def turn_back(values, start, end):
        return values * c_ref[start:end, :] - pltpu.roll(values, HS // 2, axis=1) * s_ref[
            start:end, :
        ]

    for start in range(0, tokens, rows):
        end = start + rows
        query, grad = q_ref[start:end, :], g_ref[start:end, :]
        keys, values = k_ref[:end, :], v_ref[:end, :]
        share = jnp.exp(causal_scores(query, keys, start) - lse_ref[start:end, :1])
        share_grad = dot_nt(grad, values)
        mean = jnp.sum(share_grad * share, axis=-1, keepdims=True)
        score_grad = (share * (share_grad - mean)).astype(BF)
        dv_ref[:end, :] += dot_tn(share.astype(BF), grad)
        dk_ref[:end, :] += dot_tn(score_grad, query)
        query_grad = turn_back(dot(score_grad, keys), start, end) * (HS**-0.5)
        out_ref[start:end, pl.ds(pl.multiple_of(place, HS), HS)] = query_grad.astype(BF)
    place_k = pl.multiple_of(place + heads * HS, HS)
    place_v = pl.multiple_of(place + 2 * heads * HS, HS)
    out_ref[:, pl.ds(place_k, HS)] = turn_back(dk_ref[...], 0, tokens).astype(BF)
    out_ref[:, pl.ds(place_v, HS)] = dv_ref[...].astype(BF)


def attend_back(query, key, value, grad, lse, tables):
    tokens, head_cols = query.shape
    heads = head_cols // HS
    spec = pl.BlockSpec((tokens, HS), lambda h: (0, h))
    out = shape_of((tokens, 3 * head_cols), BF)
    return kernel_call(
        functools.partial(attend_back_body, min(256, tokens), heads),
        (heads,),
        [spec] * 5 + [whole(tables[0]), whole(tables[1])],
        [(out, pl.BlockSpec(out.shape, lambda h: (0, 0)))],
        (query, key, value, grad, lse, *tables),
        6 * tokens * tokens * head_cols,
        scratch=[pltpu.VMEM((tokens, HS), F32)] * 2,
    )[0]


def column_blocks(array, size):
    return pl.BlockSpec((array.shape[0], size), lambda j: (0, j))


def row_blocks(array, size):
    return pl.BlockSpec((size, array.shape[1]), lambda j: (j, 0))


def gate_body(rows, count, x_ref, *refs):
    gates, ups = refs[:count], refs[count : 2 * count]
    hid_ref, gate_ref, up_ref = refs[2 * count :]
    for start in range(0, x_ref.shape[0], rows):
        part = slice(start, start + rows)
        gate = dot_parts(x_ref[part, :], [ref[...] for ref in gates])
        up = dot_parts(x_ref[part, :], [ref[...] for ref in ups])
        hid_ref[part, :] = (gate / (1.0 + jnp.exp(-gate)) * up).astype(BF)
        gate_ref[part, :] = gate.astype(BF)
        up_ref[part, :] = up.astype(BF)


def gate_up(tokens, gates, ups):
    count, size = gates[0].shape[1], 256
    shape = shape_of((tokens.shape[0], count), BF)
    out = (shape, column_blocks(shape, size))
    return kernel_call(
        functools.partial(gate_body, min(256, tokens.shape[0]), len(gates)),
        (count // size,),
        [whole(tokens)] + [column_blocks(part, size) for part in (*gates, *ups)],
        [out, out, out],
        (tokens, *gates, *ups),
        4 * tokens.size * count,
    )


def over_in_body(transposed, left_ref, *refs):
    refs[-1][...] = dot_parts(left_ref[...], [ref[...] for ref in refs[:-1]], transposed).astype(BF)


def over_in(left, parts, transposed):
    size = 256
    blocks = row_blocks if transposed else column_blocks
    count = parts[0].shape[0 if transposed else 1]
    shape = shape_of((left.shape[0], count), BF)
    return kernel_call(
        functools.partial(over_in_body, transposed),
        (count // size,),
        [whole(left)] + [blocks(part, size) for part in parts],
        [(shape, column_blocks(shape, size))],
        (left, *parts),
        2 * left.size * count,
    )[0]


def over_out_body(transposed, lefts, steps, *refs):
    parts = (len(refs) - 1 - lefts) // lefts
    for part in range(parts):

        @pl.when(pl.program_id(0) // steps == part)
        def _():
            total = None
            for i in range(lefts):
                right = refs[lefts + i * parts + part][...]
                got = (dot_nt if transposed else dot)(refs[i][...], right)
                total = got if total is None else total + got
            refs[-1][...] = total.astype(BF)


def over_out(lefts, rights, transposed):
    size = 256
    free = 0 if transposed else 1
    steps = rights[0][0].shape[free] // size
    count = steps * len(rights[0])
    specs = []
    for parts in rights:
        for i, part in enumerate(parts):
            block = (size, part.shape[1]) if transposed else (part.shape[0], size)

            def place(j, i=i):
                at = jnp.clip(j - i * steps, 0, steps - 1)
                return (at, 0) if transposed else (0, at)

            specs.append(pl.BlockSpec(block, place))
    shape = shape_of((lefts[0].shape[0], count * size), BF)
    return kernel_call(
        functools.partial(over_out_body, transposed, len(lefts), steps),
        (count,),
        [whole(left) for left in lefts] + specs,
        [(shape, column_blocks(shape, size))],
        (*lefts, *(part for parts in rights for part in parts)),
        sum(2 * left.size for left in lefts) * count * size,
    )[0]


def hidden_back_body(rows, count, y_ref, *refs):
    gate_ref, up_ref, dg_ref, du_ref = refs[count:]
    for start in range(0, y_ref.shape[0], rows):
        part = slice(start, start + rows)
        grad = dot_parts(y_ref[part, :], [ref[...] for ref in refs[:count]], True)
        gate, up = gate_ref[part, :].astype(F32), up_ref[part, :].astype(F32)
        sigmoid = 1.0 / (1.0 + jnp.exp(-gate))
        dg_ref[part, :] = (grad * up * sigmoid * (1.0 + gate * (1.0 - sigmoid))).astype(BF)
        du_ref[part, :] = (grad * (gate * sigmoid)).astype(BF)


def hidden_back(grad, downs, gate, up):
    count, size = downs[0].shape[0], 256
    shape = shape_of((grad.shape[0], count), BF)
    out = (shape, column_blocks(shape, size))
    return kernel_call(
        functools.partial(hidden_back_body, min(256, grad.shape[0]), len(downs)),
        (count // size,),
        [whole(grad)]
        + [row_blocks(part, size) for part in downs]
        + [column_blocks(gate, size), column_blocks(up, size)],
        [out, out],
        (grad, *downs, gate, up),
        2 * grad.size * count,
    )


ROWS = 64


def rows_call(body, scalars, arrays, outs):
    rows, width = arrays[0].shape
    size = min(ROWS, rows)
    spec = pl.BlockSpec((size, width), lambda i: (i, 0))
    out = []
    for shape, dtype in outs:
        block = (8, 128) if shape[1] == 128 else (size, width)
        out.append((shape_of(shape, dtype), pl.BlockSpec(block, lambda i: (i, 0))))
    return kernel_call(
        body,
        (rows // size,),
        [pl.BlockSpec(memory_space=pltpu.SMEM)] * len(scalars) + [spec] * len(arrays),
        out,
        (*scalars, *arrays),
        10 * rows * width,
        limit=32,
    )


def block_at(from_ref, slot, width):
    return pl.ds(pl.multiple_of(from_ref[slot] * width, 128), width)


def enter_body(from_ref, x_ref, rows_ref, normed_ref):
    count = from_ref.shape[0]
    width = x_ref.shape[1] // count
    for slot in range(count):
        here = slice(slot * width, (slot + 1) * width)
        rows_ref[:, here] = x_ref[:, block_at(from_ref, slot, width)]
    normed_ref[...] = statistics(rows_ref[...].astype(F32))[0].astype(BF)


def add_norm_body(x_ref, part_ref, sum_ref, normed_ref):
    total = x_ref[...].astype(F32) + part_ref[...].astype(F32)
    sum_ref[...] = total
    normed_ref[...] = statistics(total)[0].astype(BF)


def loss_body(
    from_ref, length_ref, scale_ref, r_ref, part_ref, t_ref, out_ref, grad_ref, low_ref, sq_ref
):
    count = from_ref.shape[0]
    width = t_ref.shape[1] // count
    size = r_ref.shape[0]
    row = pl.program_id(0) * size + lax.broadcasted_iota(jnp.int32, (size, width), 0)
    valid = row < length_ref[0]
    squares = jnp.zeros((size, width), F32)
    for slot in range(count):
        here = slice(slot * width, (slot + 1) * width)
        there = block_at(from_ref, slot, width)
        result = r_ref[:, here] + part_ref[:, here].astype(F32)
        out_ref[:, there] = result.astype(BF)
        error = jnp.where(valid, result - t_ref[:, there].astype(F32), 0.0)
        squares += error * error
        grad = error * scale_ref[0]
        grad_ref[:, here] = grad
        low_ref[:, here] = grad.astype(BF)
    sq_ref[...] = jnp.full(sq_ref.shape, jnp.sum(squares), F32)


def middle_back_body(grad_ref, r_ref, part_ref, out_ref, low_ref):
    total = grad_ref[...] + norm_back(r_ref[...], part_ref[...].astype(F32))
    out_ref[...] = total
    low_ref[...] = total.astype(BF)


def leave_body(from_ref, x_ref, grad_ref, part_ref, out_ref):
    count = from_ref.shape[0]
    width = x_ref.shape[1] // count
    total = grad_ref[...] + norm_back(x_ref[...].astype(F32), part_ref[...].astype(F32))
    for slot in range(count):
        out_ref[:, block_at(from_ref, slot, width)] = total[:, slot * width : (slot + 1) * width]


class PlainLinks:
    line = "tensor"
    rows = "dp"

    def sources(self):
        return jnp.zeros((1,), jnp.int32)

    def gather_x(self, shard, axis, late=()):
        return lax.all_gather(shard, "dp", axis=axis, tiled=True)

    def gather_y(self, value, axis, late=()):
        return value

    def gather_y_first(self, shard, axis):
        return shard

    def gather_x_last(self, value, axis):
        return lax.all_gather(value, "dp", axis=axis, tiled=True)

    def gather_core(self, value):
        return (value,)

    def scatter_core(self, left, right, axis):
        grad = dot_tn(left, right).astype(BF)
        return lax.psum_scatter(grad, "dp", scatter_dimension=axis, tiled=True)

    def send_y(self, grad, axis):
        return (grad,)

    def send_x(self, grad, axis):
        return (grad,)

    def send_x_first(self, grad, axis):
        return (grad,)

    def fold(self, sent):
        return sent[0].astype(F32)

    def total(self, value, everywhere):
        return lax.psum(value, ("dp", "tensor") if everywhere else "dp")


SWAP = [(0, 1), (1, 0)]


def halves(values, axis):
    size = values.shape[axis] // 2
    return (
        lax.slice_in_dim(values, 0, size, axis=axis),
        lax.slice_in_dim(values, size, 2 * size, axis=axis),
    )


class BlockLinks:
    line = "z"
    rows = ("y", "x", "core")

    def swap(self, values, axis):
        return lax.ppermute(values, axis, SWAP)

    def sources(self):
        slot = jnp.arange(8, dtype=jnp.int32)
        y, core = lax.axis_index("y"), lax.axis_index("core")
        return (y ^ (slot // 2 % 2)) * 4 + slot % 2 * 2 + (core ^ (slot // 4))

    def of_x(self, values, axis, flip=False):
        size = values.shape[axis] // 2
        place = lax.axis_index("x")
        if flip:
            place = 1 - place
        return lax.dynamic_slice_in_dim(values, place * size, size, axis=axis)

    def gather_x(self, shard, axis, late=()):
        other = after(self.swap(shard, "x"), *late)
        first = lax.axis_index("x") == 0
        return jnp.concatenate(
            [jnp.where(first, shard, other), jnp.where(first, other, shard)], axis=axis
        )

    def gather_y(self, value, axis, late=()):
        return jnp.concatenate([value, after(self.swap(value, "y"), *late)], axis=axis)

    def gather_y_first(self, shard, axis):
        return jnp.concatenate([shard, self.swap(shard, "y")], axis=axis)

    def gather_x_last(self, value, axis):
        other = self.swap(value, "x")
        first = lax.axis_index("x") == 0
        parts = []
        for own, far in zip(halves(value, axis), halves(other, axis)):
            parts += [jnp.where(first, own, far), jnp.where(first, far, own)]
        return jnp.concatenate(parts, axis=axis)

    def gather_core(self, value):
        return (value, self.swap(value, "core"))

    def scatter_core(self, left, right, axis):
        if axis == 0:
            keep, send = halves(left, 1)
            received = self.swap(dot_tn(send, right).astype(BF), "core")
            return (dot_tn(keep, right) + received.astype(F32)).astype(BF)
        keep, send = halves(right, 1)
        received = self.swap(dot_tn(left, send).astype(BF), "core")
        return (dot_tn(left, keep) + received.astype(F32)).astype(BF)

    def send_y(self, grad, axis):
        keep, send = halves(grad, axis)
        return (keep, self.swap(send, "y"))

    def send_x(self, grad, axis):
        return (self.of_x(grad, axis), self.swap(self.of_x(grad, axis, flip=True), "x"))

    def send_x_first(self, grad, axis):
        pairs = halves(grad, axis)
        send = jnp.concatenate([self.of_x(pair, axis, flip=True) for pair in pairs], axis=axis)
        keep = jnp.concatenate([self.of_x(pair, axis) for pair in pairs], axis=axis)
        return (keep, self.swap(send, "x"))

    def fold(self, sent):
        return sent[0].astype(F32) + sent[1].astype(F32)

    def total(self, value, everywhere):
        value = jnp.full((8, 128), value, F32)
        for name in self.rows:
            value = value + self.swap(value, name)
        for step in (1, 2) if everywhere else ():
            value = value + lax.ppermute(value, "z", [(i, i ^ step) for i in range(4)])
        return value[0, 0]


def tied(*values):
    return lax.optimization_barrier(values)


def after(value, *others):
    return lax.optimization_barrier((value, others))[0]


def layer(links, inputs, teacher, lengths, w_query, w_key, w_value, w_out, w_gate, w_up, w_down):
    line = links.line
    local_rows = inputs.shape[1]
    slot_count = local_rows * lax.axis_size(line)
    token_total = slot_count * lax.axis_size(links.rows)
    width_all = inputs.shape[2]
    head_cols = w_query.shape[1]

    def line_in(values):
        return lax.all_gather(values, line, axis=0, tiled=True)

    def line_out(partial):
        return lax.psum_scatter(partial, line, scatter_dimension=0, tiled=True)

    shape = inputs.shape[1:]
    low, high = (shape, BF), (shape, F32)
    places = links.sources()
    own_length = lengths[0]
    valid_total = links.total(own_length.astype(F32), False)
    scale = (token_total / valid_total).reshape(1)
    left_length = (own_length - lax.axis_index(line) * local_rows).reshape(1)
    tables = rotary_tables(slot_count, HS)
    rows_in, normed = rows_call(enter_body, (places,), (inputs[0],), (low, low))
    features = line_in(normed)

    heads_full = links.gather_x(jnp.concatenate([w_query, w_key, w_value], axis=1), 0)
    heads_full = links.gather_y(heads_full, 0)
    gate_full = links.gather_x(w_gate, 0)
    heads_full, gate_full = tied(heads_full, gate_full)
    heads_full = links.gather_core(heads_full)
    out_full = links.gather_x(w_out, 1)
    features, tables, scale = tied(features, tables, scale)
    query, key, value = project_heads(features, heads_full, tables)
    out_full = links.gather_core(links.gather_y(out_full, 1, (query,)))
    up_full = links.gather_x(w_up, 0, (query,))
    gate_full = links.gather_y(gate_full, 0)
    down_full = links.gather_y_first(w_down, 1)

    attended, lse = attend(query, key, value)
    attended, up_full = tied(attended, up_full)
    attn_out = line_out(over_out([attended], [out_full], False))
    attn_out, gate_full, down_full = tied(attn_out, gate_full, down_full)
    gate_full = links.gather_core(gate_full)
    up_full = links.gather_y(up_full, 0)
    down_full = links.gather_x_last(down_full, 1)
    residual, normed_two = rows_call(add_norm_body, (), (rows_in, attn_out), (high, low))

    features_two = line_in(normed_two)
    up_full, down_full = tied(up_full, down_full)
    up_full = links.gather_core(up_full)
    features_two, up_full = tied(features_two, up_full)
    down_full = links.gather_core(down_full)
    hidden, gate_pre, up_pre = gate_up(features_two, gate_full, up_full)
    mlp_out = line_out(over_out([hidden], [down_full], False))
    result, grad_result, grad_low, squares = rows_call(
        loss_body,
        (places, left_length, scale),
        (residual, mlp_out, teacher[0]),
        (low, high, low, ((local_rows // ROWS * 8, 128), F32)),
    )
    total_squares = links.total(jnp.sum(squares[::8, 0]), True)
    loss_value = total_squares / (valid_total * width_all)

    down_grad_in = line_in(grad_low)
    down_grad_in, loss_value = tied(down_grad_in, loss_value)
    gate_grad, up_grad = hidden_back(down_grad_in, down_full, gate_pre, up_pre)
    partial = over_out([gate_grad, up_grad], [gate_full, up_full], True)
    middle_grad = line_out(partial)
    features_two, hidden = after((features_two, hidden), partial)
    gate = links.scatter_core(features_two, gate_grad, 0)
    down = links.scatter_core(hidden, down_grad_in, 1)
    up = links.scatter_core(features_two, up_grad, 0)
    middle_grad, gate, down, up = tied(middle_grad, gate, down, up)
    gate = links.send_y(gate, 0)
    down = links.send_x_first(down, 1)
    up = links.send_y(up, 0)
    residual_grad, residual_low = rows_call(
        middle_back_body, (), (grad_result, residual, middle_grad), (high, low)
    )
    attn_grad_in = line_in(residual_low)
    attn_grad_in, gate, down = tied(attn_grad_in, gate, down)
    gate = links.send_x(links.fold(gate).astype(BF), 0)
    down = links.send_y(links.fold(down).astype(BF), 1)

    mixed_grad = over_in(attn_grad_in, out_full, True)
    heads_grad = attend_back(query, key, value, mixed_grad, lse, tables)
    heads_grad, up = tied(heads_grad, up)
    normed_grad = over_out([heads_grad], [heads_full], True)
    last = line_out(normed_grad)
    grad_heads = links.scatter_core(features, after(heads_grad, normed_grad), 0)
    cut = 2 * head_cols
    heads = links.send_y(grad_heads[:, :cut], 0)
    tail = links.send_x_first(grad_heads[:, cut:], 0)
    up = links.send_x(links.fold(after(up, grad_heads)).astype(BF), 0)
    grad_out = links.scatter_core(attended, after(attn_grad_in, grad_heads), 1)
    out = links.send_y(after(grad_out, heads), 1)
    grad_heads = links.fold(links.send_x(links.fold(heads).astype(BF), 0))
    tail = links.fold(links.send_y(links.fold(tail).astype(BF), 0))
    input_grad = rows_call(leave_body, (places,), (rows_in, residual_grad, last), (high,))[0]
    return (
        result[None],
        loss_value,
        input_grad[None],
        grad_heads[:, :head_cols],
        grad_heads[:, head_cols:],
        tail,
        links.fold(links.send_x(links.fold(out).astype(BF), 1)),
        links.fold(gate),
        links.fold(up),
        links.fold(down),
    )


def solution(mesh):
    if mesh.shape["dp"] == 8 and mesh.shape["tensor"] == 4:
        links = BlockLinks()
        mesh = Mesh(mesh.devices.reshape(2, 2, 2, 4), ("y", "x", "core", "z"))
    else:
        links = PlainLinks()
    dp, tensor = links.rows, links.line
    tokens = P(dp, tensor, None)
    rows = P(dp, tensor)
    cols = P(tensor, dp)
    in_specs = (tokens, tokens, P(dp), rows, rows, rows, cols, rows, rows, cols)
    out_specs = (tokens, P(), tokens, rows, rows, rows, cols, rows, rows, cols)

    def local(*args):
        return layer(links, *args)

    return jax.shard_map(
        local, mesh=mesh, in_specs=in_specs, out_specs=out_specs, check_vma=False
    )
```

```python
import functools
import math

import jax
import jax.numpy as jnp
from jax import lax
from jax.experimental import pallas as pl
from jax.experimental.pallas import tpu as pltpu
from jax.sharding import Mesh
from jax.sharding import PartitionSpec as P

HS = 128
EPSILON = 1e-05
BF = jnp.bfloat16
F32 = jnp.float32
NEGATIVE = -1e30


def statistics(values):
    centre = values - jnp.mean(values, axis=-1, keepdims=True)
    spread = jnp.mean(centre * centre, axis=-1, keepdims=True)
    inverse = lax.rsqrt(spread + EPSILON)
    return centre * inverse, inverse


def norm_back(values, grad_in):
    normed, inverse = statistics(values)
    return inverse * (
        grad_in
        - jnp.mean(grad_in, axis=-1, keepdims=True)
        - normed * jnp.mean(grad_in * normed, axis=-1, keepdims=True)
    )


def rotary_tables(length, size):
    half_size = size // 2
    inverse = jnp.exp(jnp.arange(half_size, dtype=F32) * (-2.0 * math.log(10000.0) / size))
    angles = jnp.arange(length, dtype=F32)[:, None] * inverse[None, :]
    cosine, sine = jnp.cos(angles), jnp.sin(angles)
    return (
        jnp.concatenate([cosine, cosine], axis=1),
        jnp.concatenate([-sine, sine], axis=1),
    )


def dot(left, right):
    return jnp.dot(left, right, preferred_element_type=F32)


def dot_nt(left, right):
    return lax.dot_general(left, right, (((1,), (1,)), ((), ())), preferred_element_type=F32)


def dot_tn(left, right):
    return lax.dot_general(left, right, (((0,), (0,)), ((), ())), preferred_element_type=F32)


def kernel_call(body, grid, ins, outs, args, flops, scratch=(), limit=48):
    args = tuple(
        pltpu.with_memory_space_constraint(a, pltpu.HBM) if a.size > 1024 else a for a in args
    )
    moved = sum(a.size * a.dtype.itemsize for a in args)
    moved += sum(math.prod(shape.shape) * shape.dtype.itemsize for shape, _ in outs)
    return pl.pallas_call(
        body,
        grid=grid,
        in_specs=ins,
        out_specs=[spec for _, spec in outs],
        out_shape=[pltpu.HBM(shape.shape, shape.dtype) for shape, _ in outs],
        scratch_shapes=list(scratch),
        compiler_params=pltpu.CompilerParams(
            dimension_semantics=("arbitrary",) * len(grid), vmem_limit_bytes=limit << 20
        ),
        cost_estimate=pl.CostEstimate(flops=flops, transcendentals=0, bytes_accessed=moved),
    )(*args)


def whole(array):
    rank = len(array.shape)
    return pl.BlockSpec(array.shape, lambda *_: (0,) * rank, pipeline_mode=pl.Buffered(1))


def shape_of(shape, dtype):
    return jax.ShapeDtypeStruct(shape, dtype)


def dot_parts(left, parts, transposed=False):
    total, start = None, 0
    for part in parts:
        depth = part.shape[1 if transposed else 0]
        got = (dot_nt if transposed else dot)(left[:, start : start + depth], part)
        total = got if total is None else total + got
        start += depth
    return total


def in_order(from_ref, x_ref):
    count = from_ref.shape[0]
    width = x_ref.shape[1] // count
    parts = [x_ref[:, block_at(from_ref, slot, width)] for slot in range(count)]
    return jnp.concatenate(parts, axis=1).astype(F32)


def heads_body(head_cols, count, from_ref, x_ref, *refs):
    weights = refs[:count]
    c_ref, s_ref, f_ref, q_ref, k_ref, v_ref = refs[count:]
    rows = statistics(in_order(from_ref, x_ref))[0].astype(BF)
    f_ref[...] = rows
    cosine, sine = c_ref[...], s_ref[...]
    for part, out_ref in enumerate((q_ref, k_ref, v_ref)):
        cols = slice(part * head_cols, (part + 1) * head_cols)
        got = dot_parts(rows, [w_ref[:, cols] for w_ref in weights])
        if part == 2:
            out_ref[...] = got.astype(BF)
            continue
        for start in range(0, head_cols, HS):
            head = got[:, start : start + HS]
            turned = head * cosine + pltpu.roll(head, HS // 2, axis=1) * sine
            if part == 0:
                turned = turned * (HS**-0.5)
            out_ref[:, start : start + HS] = turned.astype(BF)


def project_heads(places, states, weights, tables):
    tokens, width = states.shape
    head_cols = weights[0].shape[1] // 3
    rows = min(256, tokens)
    row_spec = pl.BlockSpec((rows, width), lambda i: (i, 0))
    table_spec = pl.BlockSpec((rows, HS), lambda i: (i, 0))
    out_spec = pl.BlockSpec((rows, head_cols), lambda i: (i, 0))
    out = (shape_of((tokens, head_cols), BF), out_spec)
    return kernel_call(
        functools.partial(heads_body, head_cols, len(weights)),
        (tokens // rows,),
        [pl.BlockSpec(memory_space=pltpu.SMEM), row_spec]
        + [*map(whole, weights), table_spec, table_spec],
        [(shape_of((tokens, width), BF), row_spec), out, out, out],
        (places, states, *weights, *tables),
        2 * tokens * width * 3 * head_cols,
    )


def residual_body(count, from_ref, x_ref, o_ref, *refs):
    weights = refs[:count]
    r_ref, b_ref = refs[count:]
    depth = o_ref.shape[2]
    total = []
    for w_ref in weights:
        part = None
        for z in range(o_ref.shape[0]):
            got = dot(o_ref[z], w_ref[z * depth : (z + 1) * depth, :])
            part = got if part is None else part + got
        total.append(part)
    total = in_order(from_ref, x_ref) + jnp.concatenate(total, axis=1)
    r_ref[...] = total
    b_ref[...] = statistics(total)[0].astype(BF)


def residual_rows(places, states, attended, weights):
    tokens, width = states.shape
    rows = min(256, tokens)
    row_spec = pl.BlockSpec((rows, width), lambda i: (i, 0))
    line, _, cols = attended.shape
    return kernel_call(
        functools.partial(residual_body, len(weights)),
        (tokens // rows,),
        [pl.BlockSpec(memory_space=pltpu.SMEM), row_spec]
        + [pl.BlockSpec((line, rows, cols), lambda i: (0, i, 0)), *map(whole, weights)],
        [(shape_of((tokens, width), F32), row_spec), (shape_of((tokens, width), BF), row_spec)],
        (places, states, attended, *weights),
        2 * tokens * width * line * cols,
    )


def causal_scores(query, keys, start):
    scores = dot_nt(query, keys)
    row = start + lax.broadcasted_iota(jnp.int32, scores.shape, 0)
    return jnp.where(row >= lax.broadcasted_iota(jnp.int32, scores.shape, 1), scores, NEGATIVE)


def attend_body(rows, q_ref, k_ref, v_ref, o_ref, lse_ref):
    for start in range(0, q_ref.shape[0], rows):
        end = start + rows
        scores = causal_scores(q_ref[start:end, :], k_ref[:end, :], start)
        largest = jnp.max(scores, axis=-1, keepdims=True)
        shifted = jnp.exp(scores - largest)
        total = jnp.sum(shifted, axis=-1, keepdims=True)
        share = (shifted * (1.0 / total)).astype(BF)
        o_ref[start:end, :] = dot(share, v_ref[:end, :]).astype(BF)
        lse_ref[start:end, :] = jnp.broadcast_to(largest + jnp.log(total), (rows, HS))


def attend(query, key, value):
    tokens, head_cols = query.shape
    spec = pl.BlockSpec((tokens, HS), lambda h: (0, h))
    return kernel_call(
        functools.partial(attend_body, min(256, tokens)),
        (head_cols // HS,),
        [spec] * 3,
        [(shape_of((tokens, head_cols), BF), spec), (shape_of((tokens, head_cols), F32), spec)],
        (query, key, value),
        3 * tokens * tokens * head_cols,
    )


def attend_back_body(
    rows, heads, q_ref, k_ref, v_ref, g_ref, lse_ref, c_ref, s_ref, out_ref, dk_ref, dv_ref
):
    tokens = q_ref.shape[0]
    place = pl.program_id(0) * HS
    dk_ref[...] = jnp.zeros_like(dk_ref)
    dv_ref[...] = jnp.zeros_like(dv_ref)

    def turn_back(values, start, end):
        return values * c_ref[start:end, :] - pltpu.roll(values, HS // 2, axis=1) * s_ref[
            start:end, :
        ]

    for start in range(0, tokens, rows):
        end = start + rows
        query, grad = q_ref[start:end, :], g_ref[start:end, :]
        keys, values = k_ref[:end, :], v_ref[:end, :]
        share = jnp.exp(causal_scores(query, keys, start) - lse_ref[start:end, :1])
        share_grad = dot_nt(grad, values)
        mean = jnp.sum(share_grad * share, axis=-1, keepdims=True)
        score_grad = (share * (share_grad - mean)).astype(BF)
        dv_ref[:end, :] += dot_tn(share.astype(BF), grad)
        dk_ref[:end, :] += dot_tn(score_grad, query)
        query_grad = turn_back(dot(score_grad, keys), start, end) * (HS**-0.5)
        out_ref[start:end, pl.ds(pl.multiple_of(place, HS), HS)] = query_grad.astype(BF)
    place_k = pl.multiple_of(place + heads * HS, HS)
    place_v = pl.multiple_of(place + 2 * heads * HS, HS)
    out_ref[:, pl.ds(place_k, HS)] = turn_back(dk_ref[...], 0, tokens).astype(BF)
    out_ref[:, pl.ds(place_v, HS)] = dv_ref[...].astype(BF)


def attend_back(query, key, value, grad, lse, tables):
    tokens, head_cols = query.shape
    heads = head_cols // HS
    spec = pl.BlockSpec((tokens, HS), lambda h: (0, h))
    out = shape_of((tokens, 3 * head_cols), BF)
    return kernel_call(
        functools.partial(attend_back_body, min(256, tokens), heads),
        (heads,),
        [spec] * 5 + [whole(tables[0]), whole(tables[1])],
        [(out, pl.BlockSpec(out.shape, lambda h: (0, 0)))],
        (query, key, value, grad, lse, *tables),
        6 * tokens * tokens * head_cols,
        scratch=[pltpu.VMEM((tokens, HS), F32)] * 2,
    )[0]


def column_blocks(array, size):
    return pl.BlockSpec((array.shape[0], size), lambda j: (0, j))


def row_blocks(array, size):
    return pl.BlockSpec((size, array.shape[1]), lambda j: (j, 0))


def gate_body(rows, count, x_ref, *refs):
    gates, ups = refs[:count], refs[count : 2 * count]
    hid_ref, gate_ref, up_ref = refs[2 * count :]
    for start in range(0, x_ref.shape[0], rows):
        part = slice(start, start + rows)
        gate = dot_parts(x_ref[part, :], [ref[...] for ref in gates])
        up = dot_parts(x_ref[part, :], [ref[...] for ref in ups])
        hid_ref[part, :] = (gate / (1.0 + jnp.exp(-gate)) * up).astype(BF)
        gate_ref[part, :] = gate.astype(BF)
        up_ref[part, :] = up.astype(BF)


def gate_up(tokens, gates, ups):
    count, size = gates[0].shape[1], 256
    shape = shape_of((tokens.shape[0], count), BF)
    out = (shape, column_blocks(shape, size))
    return kernel_call(
        functools.partial(gate_body, min(256, tokens.shape[0]), len(gates)),
        (count // size,),
        [whole(tokens)] + [column_blocks(part, size) for part in (*gates, *ups)],
        [out, out, out],
        (tokens, *gates, *ups),
        4 * tokens.size * count,
    )


def over_in_body(transposed, left_ref, *refs):
    refs[-1][...] = dot_parts(left_ref[...], [ref[...] for ref in refs[:-1]], transposed).astype(BF)


def over_in(left, parts, transposed):
    size = 256
    blocks = row_blocks if transposed else column_blocks
    count = parts[0].shape[0 if transposed else 1]
    shape = shape_of((left.shape[0], count), BF)
    return kernel_call(
        functools.partial(over_in_body, transposed),
        (count // size,),
        [whole(left)] + [blocks(part, size) for part in parts],
        [(shape, column_blocks(shape, size))],
        (left, *parts),
        2 * left.size * count,
    )[0]


def over_out_body(transposed, lefts, steps, *refs):
    parts = (len(refs) - 1 - lefts) // lefts
    for part in range(parts):

        @pl.when(pl.program_id(0) // steps == part)
        def _():
            total = None
            for i in range(lefts):
                right = refs[lefts + i * parts + part][...]
                got = (dot_nt if transposed else dot)(refs[i][...], right)
                total = got if total is None else total + got
            refs[-1][...] = total.astype(BF)


def over_out(lefts, rights, transposed):
    size = 256
    free = 0 if transposed else 1
    steps = rights[0][0].shape[free] // size
    count = steps * len(rights[0])
    specs = []
    for parts in rights:
        for i, part in enumerate(parts):
            block = (size, part.shape[1]) if transposed else (part.shape[0], size)

            def place(j, i=i):
                at = jnp.clip(j - i * steps, 0, steps - 1)
                return (at, 0) if transposed else (0, at)

            specs.append(pl.BlockSpec(block, place))
    shape = shape_of((lefts[0].shape[0], count * size), BF)
    return kernel_call(
        functools.partial(over_out_body, transposed, len(lefts), steps),
        (count,),
        [whole(left) for left in lefts] + specs,
        [(shape, column_blocks(shape, size))],
        (*lefts, *(part for parts in rights for part in parts)),
        sum(2 * left.size for left in lefts) * count * size,
    )[0]


def hidden_back_body(rows, count, y_ref, *refs):
    gate_ref, up_ref, dg_ref, du_ref = refs[count:]
    for start in range(0, y_ref.shape[0], rows):
        part = slice(start, start + rows)
        grad = dot_parts(y_ref[part, :], [ref[...] for ref in refs[:count]], True)
        gate, up = gate_ref[part, :].astype(F32), up_ref[part, :].astype(F32)
        sigmoid = 1.0 / (1.0 + jnp.exp(-gate))
        dg_ref[part, :] = (grad * up * sigmoid * (1.0 + gate * (1.0 - sigmoid))).astype(BF)
        du_ref[part, :] = (grad * (gate * sigmoid)).astype(BF)


def hidden_back(grad, downs, gate, up):
    count, size = downs[0].shape[0], 256
    shape = shape_of((grad.shape[0], count), BF)
    out = (shape, column_blocks(shape, size))
    return kernel_call(
        functools.partial(hidden_back_body, min(256, grad.shape[0]), len(downs)),
        (count // size,),
        [whole(grad)]
        + [row_blocks(part, size) for part in downs]
        + [column_blocks(gate, size), column_blocks(up, size)],
        [out, out],
        (grad, *downs, gate, up),
        2 * grad.size * count,
    )


ROWS = 64


def rows_call(body, scalars, arrays, outs):
    rows, width = arrays[0].shape
    size = min(ROWS, rows)
    spec = pl.BlockSpec((size, width), lambda i: (i, 0))
    out = []
    for shape, dtype in outs:
        block = (8, 128) if shape[1] == 128 else (size, width)
        out.append((shape_of(shape, dtype), pl.BlockSpec(block, lambda i: (i, 0))))
    return kernel_call(
        body,
        (rows // size,),
        [pl.BlockSpec(memory_space=pltpu.SMEM)] * len(scalars) + [spec] * len(arrays),
        out,
        (*scalars, *arrays),
        10 * rows * width,
        limit=32,
    )


def block_at(from_ref, slot, width):
    return pl.ds(pl.multiple_of(from_ref[slot] * width, 128), width)


def loss_body(
    from_ref, length_ref, scale_ref, r_ref, part_ref, t_ref, out_ref, grad_ref, low_ref, sq_ref
):
    count = from_ref.shape[0]
    width = t_ref.shape[1] // count
    size = r_ref.shape[0]
    row = pl.program_id(0) * size + lax.broadcasted_iota(jnp.int32, (size, width), 0)
    valid = row < length_ref[0]
    squares = jnp.zeros((size, width), F32)
    for slot in range(count):
        here = slice(slot * width, (slot + 1) * width)
        there = block_at(from_ref, slot, width)
        result = r_ref[:, here] + part_ref[:, here].astype(F32)
        out_ref[:, there] = result.astype(BF)
        error = jnp.where(valid, result - t_ref[:, there].astype(F32), 0.0)
        squares += error * error
        grad = error * scale_ref[0]
        grad_ref[:, here] = grad
        low_ref[:, here] = grad.astype(BF)
    sq_ref[...] = jnp.full(sq_ref.shape, jnp.sum(squares), F32)


def middle_back_body(grad_ref, r_ref, part_ref, out_ref, low_ref):
    total = grad_ref[...] + norm_back(r_ref[...], part_ref[...].astype(F32))
    out_ref[...] = total
    low_ref[...] = total.astype(BF)


def leave_body(from_ref, x_ref, grad_ref, part_ref, out_ref):
    count = from_ref.shape[0]
    width = x_ref.shape[1] // count
    total = grad_ref[...] + norm_back(in_order(from_ref, x_ref), part_ref[...].astype(F32))
    for slot in range(count):
        out_ref[:, block_at(from_ref, slot, width)] = total[:, slot * width : (slot + 1) * width]


class PlainLinks:
    line = "tensor"
    rows = "dp"

    def sources(self):
        return jnp.zeros((1,), jnp.int32)

    def gather_x(self, shard, axis, late=()):
        return lax.all_gather(shard, "dp", axis=axis, tiled=True)

    def gather_y(self, value, axis, late=()):
        return value

    def begin_y(self, value):
        return (value,)

    def end(self, pair, axis):
        return pair[0]

    def gather_y_first(self, shard, axis):
        return shard

    def gather_x_last(self, value, axis, late=()):
        return lax.all_gather(value, "dp", axis=axis, tiled=True)

    def gather_core(self, value):
        return (value,)

    def scatter_core(self, left, right, axis):
        grad = dot_tn(left, right).astype(BF)
        return lax.psum_scatter(grad, "dp", scatter_dimension=axis, tiled=True)

    def send_y(self, grad, axis):
        return (grad,)

    def send_x(self, grad, axis):
        return (grad,)

    def send_x_first(self, grad, axis):
        return (grad,)

    def fold(self, sent):
        return sent[0].astype(F32)

    def total(self, value, everywhere):
        return lax.psum(value, ("dp", "tensor") if everywhere else "dp")


SWAP = [(0, 1), (1, 0)]


def halves(values, axis):
    size = values.shape[axis] // 2
    return (
        lax.slice_in_dim(values, 0, size, axis=axis),
        lax.slice_in_dim(values, size, 2 * size, axis=axis),
    )


class BlockLinks:
    line = "z"
    rows = ("y", "x", "core")

    def swap(self, values, axis):
        return lax.ppermute(values, axis, SWAP)

    def sources(self):
        slot = jnp.arange(8, dtype=jnp.int32)
        y, core = lax.axis_index("y"), lax.axis_index("core")
        return (y ^ (slot // 2 % 2)) * 4 + slot % 2 * 2 + (core ^ (slot // 4))

    def of_x(self, values, axis, flip=False):
        size = values.shape[axis] // 2
        place = lax.axis_index("x")
        if flip:
            place = 1 - place
        return lax.dynamic_slice_in_dim(values, place * size, size, axis=axis)

    def gather_x(self, shard, axis, late=()):
        other = after(self.swap(shard, "x"), *late)
        first = lax.axis_index("x") == 0
        return jnp.concatenate(
            [jnp.where(first, shard, other), jnp.where(first, other, shard)], axis=axis
        )

    def gather_y(self, value, axis, late=()):
        return jnp.concatenate([value, after(self.swap(value, "y"), *late)], axis=axis)

    def begin_y(self, value):
        return (value, self.swap(value, "y"))

    def end(self, pair, axis):
        return jnp.concatenate(pair, axis=axis)

    def gather_y_first(self, shard, axis):
        return jnp.concatenate([shard, self.swap(shard, "y")], axis=axis)

    def gather_x_last(self, value, axis, late=()):
        other = after(self.swap(value, "x"), *late)
        first = lax.axis_index("x") == 0
        parts = []
        for own, far in zip(halves(value, axis), halves(other, axis)):
            parts += [jnp.where(first, own, far), jnp.where(first, far, own)]
        return jnp.concatenate(parts, axis=axis)

    def gather_core(self, value):
        return (value, self.swap(value, "core"))

    def scatter_core(self, left, right, axis):
        if axis == 0:
            keep, send = halves(left, 1)
            received = self.swap(dot_tn(send, right).astype(BF), "core")
            return (dot_tn(keep, right) + received.astype(F32)).astype(BF)
        keep, send = halves(right, 1)
        received = self.swap(dot_tn(left, send).astype(BF), "core")
        return (dot_tn(left, keep) + received.astype(F32)).astype(BF)

    def send_y(self, grad, axis):
        keep, send = halves(grad, axis)
        return (keep, self.swap(send, "y"))

    def send_x(self, grad, axis):
        return (self.of_x(grad, axis), self.swap(self.of_x(grad, axis, flip=True), "x"))

    def send_x_first(self, grad, axis):
        pairs = halves(grad, axis)
        send = jnp.concatenate([self.of_x(pair, axis, flip=True) for pair in pairs], axis=axis)
        keep = jnp.concatenate([self.of_x(pair, axis) for pair in pairs], axis=axis)
        return (keep, self.swap(send, "x"))

    def fold(self, sent):
        return sent[0].astype(F32) + sent[1].astype(F32)

    def total(self, value, everywhere):
        value = jnp.full((8, 128), value, F32)
        for name in self.rows:
            value = value + self.swap(value, name)
        for step in (1, 2) if everywhere else ():
            value = value + lax.ppermute(value, "z", [(i, i ^ step) for i in range(4)])
        return value[0, 0]


def tied(*values):
    return lax.optimization_barrier(values)


def after(value, *others):
    return lax.optimization_barrier((value, others))[0]


def layer(links, inputs, teacher, lengths, w_query, w_key, w_value, w_out, w_gate, w_up, w_down):
    line = links.line
    local_rows = inputs.shape[1]
    slot_count = local_rows * lax.axis_size(line)
    token_total = slot_count * lax.axis_size(links.rows)
    width_all = inputs.shape[2]
    head_cols = w_query.shape[1]

    def line_in(values):
        return lax.all_gather(values, line, axis=0, tiled=True)

    def line_out(partial):
        return lax.psum_scatter(partial, line, scatter_dimension=0, tiled=True)

    shape = inputs.shape[1:]
    low, high = (shape, BF), (shape, F32)
    places = links.sources()
    own_length = lengths[0]
    valid_total = links.total(own_length.astype(F32), False)
    scale = (token_total / valid_total).reshape(1)
    left_length = (own_length - lax.axis_index(line) * local_rows).reshape(1)
    tables = rotary_tables(slot_count, HS)
    states = line_in(inputs[0])

    heads_full = links.gather_x(jnp.concatenate([w_query, w_key, w_value], axis=1), 0)
    heads_full = links.gather_y(heads_full, 0)
    gate_full = links.gather_x(w_gate, 0)
    heads_full, gate_full = tied(heads_full, gate_full)
    heads_full = links.gather_core(heads_full)
    down_full = links.gather_x(after(w_down, gate_full), 1)
    up_full = links.gather_y_first(w_up, 0)
    states, tables, scale, down_full, up_full = tied(states, tables, scale, down_full, up_full)
    out_full = lax.all_gather(after(w_out, states), line, axis=0, tiled=True)
    features, query, key, value = project_heads(places, states, heads_full, tables)
    gate_full = links.begin_y(gate_full)
    up_full = links.gather_x_last(up_full, 0, (query,))

    attended, lse = attend(query, key, value)
    attended, up_full, gate_full = tied(attended, up_full, gate_full)
    out_full = links.gather_y_first(after(out_full, attended), 1)
    out_full = links.gather_x_last(out_full, 1)
    down_full = links.gather_y(down_full, 1)
    gate_full = links.end(after(gate_full, attended), 0)
    everyone = lax.all_gather(attended, line, axis=0)
    everyone, out_full, down_full = tied(everyone, out_full, down_full)
    out_full = links.gather_core(out_full)
    gate_full = links.gather_core(gate_full)
    up_full = links.gather_core(up_full)
    residual, features_two = residual_rows(places, states, everyone, out_full)
    down_full = links.gather_core(after(down_full, features_two))
    place = lax.axis_index(line)
    residual = lax.dynamic_slice_in_dim(residual, place * local_rows, local_rows, axis=0)
    out_rows = tuple(
        lax.dynamic_slice_in_dim(part, place * head_cols, head_cols, axis=0) for part in out_full
    )
    hidden, gate_pre, up_pre = gate_up(features_two, gate_full, up_full)
    mlp_out = line_out(over_out([hidden], [down_full], False))
    result, grad_result, grad_low, squares = rows_call(
        loss_body,
        (places, left_length, scale),
        (residual, mlp_out, teacher[0]),
        (low, high, low, ((local_rows // ROWS * 8, 128), F32)),
    )
    total_squares = links.total(jnp.sum(squares[::8, 0]), True)
    loss_value = total_squares / (valid_total * width_all)

    down_grad_in = line_in(grad_low)
    down_grad_in, loss_value = tied(down_grad_in, loss_value)
    gate_grad, up_grad = hidden_back(down_grad_in, down_full, gate_pre, up_pre)
    partial = over_out([gate_grad, up_grad], [gate_full, up_full], True)
    middle_grad = line_out(partial)
    features_two, hidden = after((features_two, hidden), partial)
    gate = links.scatter_core(features_two, gate_grad, 0)
    down = links.scatter_core(hidden, down_grad_in, 1)
    up = links.scatter_core(features_two, up_grad, 0)
    middle_grad, gate, down, up = tied(middle_grad, gate, down, up)
    gate = links.send_y(gate, 0)
    down = links.send_x_first(down, 1)
    up = links.send_y(up, 0)
    residual_grad, residual_low = rows_call(
        middle_back_body, (), (grad_result, residual, middle_grad), (high, low)
    )
    attn_grad_in = line_in(residual_low)
    attn_grad_in, gate, down = tied(attn_grad_in, gate, down)
    gate = links.send_x(links.fold(gate).astype(BF), 0)
    down = links.send_y(links.fold(down).astype(BF), 1)

    mixed_grad = over_in(attn_grad_in, out_rows, True)
    heads_grad = attend_back(query, key, value, mixed_grad, lse, tables)
    heads_grad, up = tied(heads_grad, up)
    normed_grad = over_out([heads_grad], [heads_full], True)
    last = line_out(normed_grad)
    grad_heads = links.scatter_core(features, after(heads_grad, normed_grad), 0)
    cut = 2 * head_cols
    heads = links.send_y(grad_heads[:, :cut], 0)
    tail = links.send_x_first(grad_heads[:, cut:], 0)
    up = links.send_x(links.fold(after(up, grad_heads)).astype(BF), 0)
    grad_out = links.scatter_core(attended, after(attn_grad_in, grad_heads), 1)
    out = links.send_y(after(grad_out, heads), 1)
    grad_heads = links.fold(links.send_x(links.fold(heads).astype(BF), 0))
    tail = links.fold(links.send_y(links.fold(tail).astype(BF), 0))
    input_grad = rows_call(
        leave_body, (places,), (inputs[0], residual_grad, last), (high,)
    )[0]
    return (
        result[None],
        loss_value,
        input_grad[None],
        grad_heads[:, :head_cols],
        grad_heads[:, head_cols:],
        tail,
        links.fold(links.send_x(links.fold(out).astype(BF), 1)),
        links.fold(gate),
        links.fold(up),
        links.fold(down),
    )


def solution(mesh):
    if mesh.shape["dp"] == 8 and mesh.shape["tensor"] == 4:
        links = BlockLinks()
        mesh = Mesh(mesh.devices.reshape(2, 2, 2, 4), ("y", "x", "core", "z"))
    else:
        links = PlainLinks()
    dp, tensor = links.rows, links.line
    tokens = P(dp, tensor, None)
    rows = P(dp, tensor)
    cols = P(tensor, dp)
    in_specs = (tokens, tokens, P(dp), rows, rows, rows, cols, rows, rows, cols)
    out_specs = (tokens, P(), tokens, rows, rows, rows, cols, rows, rows, cols)

    def local(*args):
        return layer(links, *args)

    return jax.shard_map(
        local, mesh=mesh, in_specs=in_specs, out_specs=out_specs, check_vma=False
    )
```

```python
import functools
import math

import jax
import jax.numpy as jnp
from jax import lax
from jax.experimental import pallas as pl
from jax.experimental.pallas import tpu as pltpu
from jax.sharding import Mesh
from jax.sharding import PartitionSpec as P

HS = 128
EPSILON = 1e-05
BF = jnp.bfloat16
F32 = jnp.float32
NEGATIVE = -1e30


def statistics(values):
    centre = values - jnp.mean(values, axis=-1, keepdims=True)
    spread = jnp.mean(centre * centre, axis=-1, keepdims=True)
    inverse = lax.rsqrt(spread + EPSILON)
    return centre * inverse, inverse


def norm_back(values, grad_in):
    normed, inverse = statistics(values)
    return inverse * (
        grad_in
        - jnp.mean(grad_in, axis=-1, keepdims=True)
        - normed * jnp.mean(grad_in * normed, axis=-1, keepdims=True)
    )


def rotary_tables(length, size):
    half_size = size // 2
    inverse = jnp.exp(jnp.arange(half_size, dtype=F32) * (-2.0 * math.log(10000.0) / size))
    angles = jnp.arange(length, dtype=F32)[:, None] * inverse[None, :]
    cosine, sine = jnp.cos(angles), jnp.sin(angles)
    return (
        jnp.concatenate([cosine, cosine], axis=1),
        jnp.concatenate([-sine, sine], axis=1),
    )


def dot(left, right):
    return jnp.dot(left, right, preferred_element_type=F32)


def dot_nt(left, right):
    return lax.dot_general(left, right, (((1,), (1,)), ((), ())), preferred_element_type=F32)


def dot_tn(left, right):
    return lax.dot_general(left, right, (((0,), (0,)), ((), ())), preferred_element_type=F32)


def kernel_call(body, grid, ins, outs, args, flops, scratch=(), limit=48):
    args = tuple(
        pltpu.with_memory_space_constraint(a, pltpu.HBM) if a.size > 1024 else a for a in args
    )
    moved = sum(a.size * a.dtype.itemsize for a in args)
    moved += sum(math.prod(shape.shape) * shape.dtype.itemsize for shape, _ in outs)
    return pl.pallas_call(
        body,
        grid=grid,
        in_specs=ins,
        out_specs=[spec for _, spec in outs],
        out_shape=[pltpu.HBM(shape.shape, shape.dtype) for shape, _ in outs],
        scratch_shapes=list(scratch),
        compiler_params=pltpu.CompilerParams(
            dimension_semantics=("arbitrary",) * len(grid), vmem_limit_bytes=limit << 20
        ),
        cost_estimate=pl.CostEstimate(flops=flops, transcendentals=0, bytes_accessed=moved),
    )(*args)


def whole(array):
    rank = len(array.shape)
    return pl.BlockSpec(array.shape, lambda *_: (0,) * rank, pipeline_mode=pl.Buffered(1))


def shape_of(shape, dtype):
    return jax.ShapeDtypeStruct(shape, dtype)


def dot_parts(left, parts, transposed=False):
    total, start = None, 0
    for part in parts:
        depth = part.shape[1 if transposed else 0]
        got = (dot_nt if transposed else dot)(left[:, start : start + depth], part)
        total = got if total is None else total + got
        start += depth
    return total


def in_order(from_ref, x_ref):
    count = from_ref.shape[0]
    width = x_ref.shape[1] // count
    parts = [x_ref[:, block_at(from_ref, slot, width)] for slot in range(count)]
    return jnp.concatenate(parts, axis=1).astype(F32)


def heads_body(head_cols, count, from_ref, x_ref, *refs):
    weights = refs[:count]
    c_ref, s_ref, f_ref, q_ref, k_ref, v_ref = refs[count:]
    rows = statistics(in_order(from_ref, x_ref))[0].astype(BF)
    f_ref[...] = rows
    cosine, sine = c_ref[...], s_ref[...]
    for part, out_ref in enumerate((q_ref, k_ref, v_ref)):
        cols = slice(part * head_cols, (part + 1) * head_cols)
        got = dot_parts(rows, [w_ref[:, cols] for w_ref in weights])
        if part == 2:
            out_ref[...] = got.astype(BF)
            continue
        for start in range(0, head_cols, HS):
            head = got[:, start : start + HS]
            turned = head * cosine + pltpu.roll(head, HS // 2, axis=1) * sine
            if part == 0:
                turned = turned * (HS**-0.5)
            out_ref[:, start : start + HS] = turned.astype(BF)


def project_heads(places, states, weights, tables):
    tokens, width = states.shape
    head_cols = weights[0].shape[1] // 3
    rows = min(256, tokens)
    row_spec = pl.BlockSpec((rows, width), lambda i: (i, 0))
    table_spec = pl.BlockSpec((rows, HS), lambda i: (i, 0))
    out_spec = pl.BlockSpec((rows, head_cols), lambda i: (i, 0))
    out = (shape_of((tokens, head_cols), BF), out_spec)
    return kernel_call(
        functools.partial(heads_body, head_cols, len(weights)),
        (tokens // rows,),
        [pl.BlockSpec(memory_space=pltpu.SMEM), row_spec]
        + [*map(whole, weights), table_spec, table_spec],
        [(shape_of((tokens, width), BF), row_spec), out, out, out],
        (places, states, *weights, *tables),
        2 * tokens * width * 3 * head_cols,
    )


def residual_body(count, from_ref, x_ref, o_ref, *refs):
    weights = refs[:count]
    r_ref, b_ref = refs[count:]
    depth = o_ref.shape[2]
    total = []
    for w_ref in weights:
        part = None
        for z in range(o_ref.shape[0]):
            got = dot(o_ref[z], w_ref[z * depth : (z + 1) * depth, :])
            part = got if part is None else part + got
        total.append(part)
    total = in_order(from_ref, x_ref) + jnp.concatenate(total, axis=1)
    r_ref[...] = total
    b_ref[...] = statistics(total)[0].astype(BF)


def residual_rows(places, states, attended, weights):
    tokens, width = states.shape
    rows = min(256, tokens)
    row_spec = pl.BlockSpec((rows, width), lambda i: (i, 0))
    line, _, cols = attended.shape
    return kernel_call(
        functools.partial(residual_body, len(weights)),
        (tokens // rows,),
        [pl.BlockSpec(memory_space=pltpu.SMEM), row_spec]
        + [pl.BlockSpec((line, rows, cols), lambda i: (0, i, 0)), *map(whole, weights)],
        [(shape_of((tokens, width), F32), row_spec), (shape_of((tokens, width), BF), row_spec)],
        (places, states, attended, *weights),
        2 * tokens * width * line * cols,
    )


def causal_scores(query, keys, start):
    scores = dot_nt(query, keys)
    row = start + lax.broadcasted_iota(jnp.int32, scores.shape, 0)
    return jnp.where(row >= lax.broadcasted_iota(jnp.int32, scores.shape, 1), scores, NEGATIVE)


def attend_body(rows, q_ref, k_ref, v_ref, o_ref, lse_ref):
    for start in range(0, q_ref.shape[0], rows):
        end = start + rows
        scores = causal_scores(q_ref[start:end, :], k_ref[:end, :], start)
        largest = jnp.max(scores, axis=-1, keepdims=True)
        shifted = jnp.exp(scores - largest)
        total = jnp.sum(shifted, axis=-1, keepdims=True)
        share = (shifted * (1.0 / total)).astype(BF)
        o_ref[start:end, :] = dot(share, v_ref[:end, :]).astype(BF)
        lse_ref[start:end, :] = jnp.broadcast_to(largest + jnp.log(total), (rows, HS))


def attend(query, key, value):
    tokens, head_cols = query.shape
    spec = pl.BlockSpec((tokens, HS), lambda h: (0, h))
    return kernel_call(
        functools.partial(attend_body, min(256, tokens)),
        (head_cols // HS,),
        [spec] * 3,
        [(shape_of((tokens, head_cols), BF), spec), (shape_of((tokens, head_cols), F32), spec)],
        (query, key, value),
        3 * tokens * tokens * head_cols,
    )


def attend_back_body(
    rows, heads, q_ref, k_ref, v_ref, g_ref, lse_ref, c_ref, s_ref, out_ref, dk_ref, dv_ref
):
    tokens = q_ref.shape[0]
    place = pl.program_id(0) * HS
    dk_ref[...] = jnp.zeros_like(dk_ref)
    dv_ref[...] = jnp.zeros_like(dv_ref)

    def turn_back(values, start, end):
        return values * c_ref[start:end, :] - pltpu.roll(values, HS // 2, axis=1) * s_ref[
            start:end, :
        ]

    for start in range(0, tokens, rows):
        end = start + rows
        query, grad = q_ref[start:end, :], g_ref[start:end, :]
        keys, values = k_ref[:end, :], v_ref[:end, :]
        share = jnp.exp(causal_scores(query, keys, start) - lse_ref[start:end, :1])
        share_grad = dot_nt(grad, values)
        mean = jnp.sum(share_grad * share, axis=-1, keepdims=True)
        score_grad = (share * (share_grad - mean)).astype(BF)
        dv_ref[:end, :] += dot_tn(share.astype(BF), grad)
        dk_ref[:end, :] += dot_tn(score_grad, query)
        query_grad = turn_back(dot(score_grad, keys), start, end) * (HS**-0.5)
        out_ref[start:end, pl.ds(pl.multiple_of(place, HS), HS)] = query_grad.astype(BF)
    place_k = pl.multiple_of(place + heads * HS, HS)
    place_v = pl.multiple_of(place + 2 * heads * HS, HS)
    out_ref[:, pl.ds(place_k, HS)] = turn_back(dk_ref[...], 0, tokens).astype(BF)
    out_ref[:, pl.ds(place_v, HS)] = dv_ref[...].astype(BF)


def attend_back(query, key, value, grad, lse, tables):
    tokens, head_cols = query.shape
    heads = head_cols // HS
    spec = pl.BlockSpec((tokens, HS), lambda h: (0, h))
    out = shape_of((tokens, 3 * head_cols), BF)
    return kernel_call(
        functools.partial(attend_back_body, min(256, tokens), heads),
        (heads,),
        [spec] * 5 + [whole(tables[0]), whole(tables[1])],
        [(out, pl.BlockSpec(out.shape, lambda h: (0, 0)))],
        (query, key, value, grad, lse, *tables),
        6 * tokens * tokens * head_cols,
        scratch=[pltpu.VMEM((tokens, HS), F32)] * 2,
    )[0]


def column_blocks(array, size):
    return pl.BlockSpec((array.shape[0], size), lambda j: (0, j))


def row_blocks(array, size):
    return pl.BlockSpec((size, array.shape[1]), lambda j: (j, 0))


def gate_body(rows, count, x_ref, *refs):
    gates, ups = refs[:count], refs[count : 2 * count]
    hid_ref, gate_ref, up_ref = refs[2 * count :]
    for start in range(0, x_ref.shape[0], rows):
        part = slice(start, start + rows)
        gate = dot_parts(x_ref[part, :], [ref[...] for ref in gates])
        up = dot_parts(x_ref[part, :], [ref[...] for ref in ups])
        hid_ref[part, :] = (gate / (1.0 + jnp.exp(-gate)) * up).astype(BF)
        gate_ref[part, :] = gate.astype(BF)
        up_ref[part, :] = up.astype(BF)


def gate_up(tokens, gates, ups):
    count, size = gates[0].shape[1], 256
    shape = shape_of((tokens.shape[0], count), BF)
    out = (shape, column_blocks(shape, size))
    return kernel_call(
        functools.partial(gate_body, min(256, tokens.shape[0]), len(gates)),
        (count // size,),
        [whole(tokens)] + [column_blocks(part, size) for part in (*gates, *ups)],
        [out, out, out],
        (tokens, *gates, *ups),
        4 * tokens.size * count,
    )


def over_in_body(transposed, left_ref, *refs):
    refs[-1][...] = dot_parts(left_ref[...], [ref[...] for ref in refs[:-1]], transposed).astype(BF)


def over_in(left, parts, transposed):
    size = 256
    blocks = row_blocks if transposed else column_blocks
    count = parts[0].shape[0 if transposed else 1]
    shape = shape_of((left.shape[0], count), BF)
    return kernel_call(
        functools.partial(over_in_body, transposed),
        (count // size,),
        [whole(left)] + [blocks(part, size) for part in parts],
        [(shape, column_blocks(shape, size))],
        (left, *parts),
        2 * left.size * count,
    )[0]


def over_out_body(transposed, lefts, steps, *refs):
    parts = (len(refs) - 1 - lefts) // lefts
    for part in range(parts):

        @pl.when(pl.program_id(0) // steps == part)
        def _():
            total = None
            for i in range(lefts):
                right = refs[lefts + i * parts + part][...]
                got = (dot_nt if transposed else dot)(refs[i][...], right)
                total = got if total is None else total + got
            refs[-1][...] = total.astype(BF)


def over_out(lefts, rights, transposed):
    size = 256
    free = 0 if transposed else 1
    steps = rights[0][0].shape[free] // size
    count = steps * len(rights[0])
    specs = []
    for parts in rights:
        for i, part in enumerate(parts):
            block = (size, part.shape[1]) if transposed else (part.shape[0], size)

            def place(j, i=i):
                at = jnp.clip(j - i * steps, 0, steps - 1)
                return (at, 0) if transposed else (0, at)

            specs.append(pl.BlockSpec(block, place))
    shape = shape_of((lefts[0].shape[0], count * size), BF)
    return kernel_call(
        functools.partial(over_out_body, transposed, len(lefts), steps),
        (count,),
        [whole(left) for left in lefts] + specs,
        [(shape, column_blocks(shape, size))],
        (*lefts, *(part for parts in rights for part in parts)),
        sum(2 * left.size for left in lefts) * count * size,
    )[0]


def hidden_back_body(rows, count, y_ref, *refs):
    gate_ref, up_ref, dg_ref, du_ref = refs[count:]
    for start in range(0, y_ref.shape[0], rows):
        part = slice(start, start + rows)
        grad = dot_parts(y_ref[part, :], [ref[...] for ref in refs[:count]], True)
        gate, up = gate_ref[part, :].astype(F32), up_ref[part, :].astype(F32)
        sigmoid = 1.0 / (1.0 + jnp.exp(-gate))
        dg_ref[part, :] = (grad * up * sigmoid * (1.0 + gate * (1.0 - sigmoid))).astype(BF)
        du_ref[part, :] = (grad * (gate * sigmoid)).astype(BF)


def hidden_back(grad, downs, gate, up):
    count, size = downs[0].shape[0], 256
    shape = shape_of((grad.shape[0], count), BF)
    out = (shape, column_blocks(shape, size))
    return kernel_call(
        functools.partial(hidden_back_body, min(256, grad.shape[0]), len(downs)),
        (count // size,),
        [whole(grad)]
        + [row_blocks(part, size) for part in downs]
        + [column_blocks(gate, size), column_blocks(up, size)],
        [out, out],
        (grad, *downs, gate, up),
        2 * grad.size * count,
    )


ROWS = 64


def rows_call(body, scalars, arrays, outs):
    rows, width = arrays[0].shape
    size = min(ROWS, rows)
    spec = pl.BlockSpec((size, width), lambda i: (i, 0))
    out = []
    for shape, dtype in outs:
        block = (8, 128) if shape[1] == 128 else (size, width)
        out.append((shape_of(shape, dtype), pl.BlockSpec(block, lambda i: (i, 0))))
    return kernel_call(
        body,
        (rows // size,),
        [pl.BlockSpec(memory_space=pltpu.SMEM)] * len(scalars) + [spec] * len(arrays),
        out,
        (*scalars, *arrays),
        10 * rows * width,
        limit=32,
    )


def block_at(from_ref, slot, width):
    return pl.ds(pl.multiple_of(from_ref[slot] * width, 128), width)


def loss_body(
    from_ref, length_ref, scale_ref, r_ref, part_ref, t_ref, out_ref, grad_ref, low_ref, sq_ref
):
    count = from_ref.shape[0]
    width = t_ref.shape[1] // count
    size = r_ref.shape[0]
    row = pl.program_id(0) * size + lax.broadcasted_iota(jnp.int32, (size, width), 0)
    valid = row < length_ref[0]
    squares = jnp.zeros((size, width), F32)
    for slot in range(count):
        here = slice(slot * width, (slot + 1) * width)
        there = block_at(from_ref, slot, width)
        result = r_ref[:, here] + part_ref[:, here].astype(F32)
        out_ref[:, there] = result.astype(BF)
        error = jnp.where(valid, result - t_ref[:, there].astype(F32), 0.0)
        squares += error * error
        grad = error * scale_ref[0]
        grad_ref[:, here] = grad
        low_ref[:, here] = grad.astype(BF)
    sq_ref[...] = jnp.full(sq_ref.shape, jnp.sum(squares), F32)


def middle_back_body(grad_ref, r_ref, part_ref, out_ref, low_ref):
    total = grad_ref[...] + norm_back(r_ref[...], part_ref[...].astype(F32))
    out_ref[...] = total
    low_ref[...] = total.astype(BF)


def leave_body(from_ref, x_ref, grad_ref, part_ref, out_ref):
    count = from_ref.shape[0]
    width = x_ref.shape[1] // count
    total = grad_ref[...] + norm_back(in_order(from_ref, x_ref), part_ref[...].astype(F32))
    for slot in range(count):
        out_ref[:, block_at(from_ref, slot, width)] = total[:, slot * width : (slot + 1) * width]


class PlainLinks:
    line = "tensor"
    rows = "dp"

    def sources(self):
        return jnp.zeros((1,), jnp.int32)

    def gather_x(self, shard, axis, late=()):
        return lax.all_gather(shard, "dp", axis=axis, tiled=True)

    def gather_y(self, value, axis, late=()):
        return value

    def begin_y(self, value):
        return (value,)

    def end(self, pair, axis):
        return pair[0]

    def gather_y_first(self, shard, axis):
        return shard

    def gather_x_last(self, value, axis, late=()):
        return lax.all_gather(value, "dp", axis=axis, tiled=True)

    def gather_core(self, value):
        return (value,)

    def scatter_core(self, left, right, axis):
        grad = dot_tn(left, right).astype(BF)
        return lax.psum_scatter(grad, "dp", scatter_dimension=axis, tiled=True)

    def send_y(self, grad, axis):
        return (grad,)

    def send_x(self, grad, axis):
        return (grad,)

    def send_x_first(self, grad, axis):
        return (grad,)

    def fold(self, sent):
        return sent[0].astype(F32)

    def total(self, value, everywhere):
        return lax.psum(value, ("dp", "tensor") if everywhere else "dp")


SWAP = [(0, 1), (1, 0)]


def halves(values, axis):
    size = values.shape[axis] // 2
    return (
        lax.slice_in_dim(values, 0, size, axis=axis),
        lax.slice_in_dim(values, size, 2 * size, axis=axis),
    )


class BlockLinks:
    line = "z"
    rows = ("y", "x", "core")

    def swap(self, values, axis):
        return lax.ppermute(values, axis, SWAP)

    def sources(self):
        slot = jnp.arange(8, dtype=jnp.int32)
        y, core = lax.axis_index("y"), lax.axis_index("core")
        return (y ^ (slot // 2 % 2)) * 4 + slot % 2 * 2 + (core ^ (slot // 4))

    def of_x(self, values, axis, flip=False):
        size = values.shape[axis] // 2
        place = lax.axis_index("x")
        if flip:
            place = 1 - place
        return lax.dynamic_slice_in_dim(values, place * size, size, axis=axis)

    def gather_x(self, shard, axis, late=()):
        other = after(self.swap(shard, "x"), *late)
        first = lax.axis_index("x") == 0
        return jnp.concatenate(
            [jnp.where(first, shard, other), jnp.where(first, other, shard)], axis=axis
        )

    def gather_y(self, value, axis, late=()):
        return jnp.concatenate([value, after(self.swap(value, "y"), *late)], axis=axis)

    def begin_y(self, value):
        return (value, self.swap(value, "y"))

    def end(self, pair, axis):
        return jnp.concatenate(pair, axis=axis)

    def gather_y_first(self, shard, axis):
        return jnp.concatenate([shard, self.swap(shard, "y")], axis=axis)

    def gather_x_last(self, value, axis, late=()):
        other = after(self.swap(value, "x"), *late)
        first = lax.axis_index("x") == 0
        parts = []
        for own, far in zip(halves(value, axis), halves(other, axis)):
            parts += [jnp.where(first, own, far), jnp.where(first, far, own)]
        return jnp.concatenate(parts, axis=axis)

    def gather_core(self, value):
        return (value, self.swap(value, "core"))

    def scatter_core(self, left, right, axis):
        if axis == 0:
            keep, send = halves(left, 1)
            received = self.swap(dot_tn(send, right).astype(BF), "core")
            return (dot_tn(keep, right) + received.astype(F32)).astype(BF)
        keep, send = halves(right, 1)
        received = self.swap(dot_tn(left, send).astype(BF), "core")
        return (dot_tn(left, keep) + received.astype(F32)).astype(BF)

    def send_y(self, grad, axis):
        keep, send = halves(grad, axis)
        return (keep, self.swap(send, "y"))

    def send_x(self, grad, axis):
        return (self.of_x(grad, axis), self.swap(self.of_x(grad, axis, flip=True), "x"))

    def send_x_first(self, grad, axis):
        pairs = halves(grad, axis)
        send = jnp.concatenate([self.of_x(pair, axis, flip=True) for pair in pairs], axis=axis)
        keep = jnp.concatenate([self.of_x(pair, axis) for pair in pairs], axis=axis)
        return (keep, self.swap(send, "x"))

    def fold(self, sent):
        return sent[0].astype(F32) + sent[1].astype(F32)

    def total(self, value, everywhere):
        value = jnp.full((8, 128), value, F32)
        for name in self.rows:
            value = value + self.swap(value, name)
        for step in (1, 2) if everywhere else ():
            value = value + lax.ppermute(value, "z", [(i, i ^ step) for i in range(4)])
        return value[0, 0]


def tied(*values):
    return lax.optimization_barrier(values)


def after(value, *others):
    return lax.optimization_barrier((value, others))[0]


def layer(links, inputs, teacher, lengths, w_query, w_key, w_value, w_out, w_gate, w_up, w_down):
    line = links.line
    local_rows = inputs.shape[1]
    slot_count = local_rows * lax.axis_size(line)
    token_total = slot_count * lax.axis_size(links.rows)
    width_all = inputs.shape[2]
    head_cols = w_query.shape[1]

    def line_in(values):
        return lax.all_gather(values, line, axis=0, tiled=True)

    def line_out(partial):
        return lax.psum_scatter(partial, line, scatter_dimension=0, tiled=True)

    shape = inputs.shape[1:]
    low, high = (shape, BF), (shape, F32)
    places = links.sources()
    own_length = lengths[0]
    valid_total = links.total(own_length.astype(F32), False)
    scale = (token_total / valid_total).reshape(1)
    left_length = (own_length - lax.axis_index(line) * local_rows).reshape(1)
    tables = rotary_tables(slot_count, HS)
    states = line_in(inputs[0])

    heads_full = links.gather_x(jnp.concatenate([w_query, w_key, w_value], axis=1), 0)
    heads_full = links.gather_y(heads_full, 0)
    gate_full = links.gather_x(w_gate, 0)
    down_full = links.gather_x(after(w_down, gate_full), 1)
    heads_full, gate_full = tied(heads_full, gate_full)
    heads_full = links.gather_core(heads_full)
    up_full = links.gather_y_first(w_up, 0)
    states, tables, scale, down_full, up_full = tied(states, tables, scale, down_full, up_full)
    out_full = lax.all_gather(after(w_out, states), line, axis=0, tiled=True)
    features, query, key, value = project_heads(places, states, heads_full, tables)
    gate_full = links.begin_y(gate_full)
    up_full = links.gather_x_last(up_full, 0, (query,))

    attended, lse = attend(query, key, value)
    attended, up_full, gate_full = tied(attended, up_full, gate_full)
    out_full = links.gather_y_first(after(out_full, attended), 1)
    out_full = links.gather_x_last(out_full, 1)
    down_full = links.gather_y(down_full, 1)
    gate_full = links.end(after(gate_full, attended), 0)
    everyone = lax.all_gather(attended, line, axis=0)
    everyone, out_full, down_full = tied(everyone, out_full, down_full)
    out_full = links.gather_core(out_full)
    gate_full = links.gather_core(gate_full)
    up_full = links.gather_core(up_full)
    residual, features_two = residual_rows(places, states, everyone, out_full)
    down_full = links.gather_core(after(down_full, features_two))
    place = lax.axis_index(line)
    residual = lax.dynamic_slice_in_dim(residual, place * local_rows, local_rows, axis=0)
    out_rows = tuple(
        lax.dynamic_slice_in_dim(part, place * head_cols, head_cols, axis=0) for part in out_full
    )
    hidden, gate_pre, up_pre = gate_up(features_two, gate_full, up_full)
    mlp_out = line_out(over_out([hidden], [down_full], False))
    result, grad_result, grad_low, squares = rows_call(
        loss_body,
        (places, left_length, scale),
        (residual, mlp_out, teacher[0]),
        (low, high, low, ((local_rows // ROWS * 8, 128), F32)),
    )
    total_squares = links.total(jnp.sum(squares[::8, 0]), True)
    loss_value = total_squares / (valid_total * width_all)

    down_grad_in = line_in(grad_low)
    down_grad_in, loss_value = tied(down_grad_in, loss_value)
    gate_grad, up_grad = hidden_back(down_grad_in, down_full, gate_pre, up_pre)
    partial = over_out([gate_grad, up_grad], [gate_full, up_full], True)
    middle_grad = line_out(partial)
    features_two, hidden = after((features_two, hidden), partial)
    gate = links.scatter_core(features_two, gate_grad, 0)
    down = links.scatter_core(hidden, down_grad_in, 1)
    up = links.scatter_core(features_two, up_grad, 0)
    middle_grad, gate, down, up = tied(middle_grad, gate, down, up)
    gate = links.send_y(gate, 0)
    down = links.send_x_first(down, 1)
    up = links.send_y(up, 0)
    residual_grad, residual_low = rows_call(
        middle_back_body, (), (grad_result, residual, middle_grad), (high, low)
    )
    attn_grad_in = line_in(residual_low)
    attn_grad_in, gate, down = tied(attn_grad_in, gate, down)
    gate = links.send_x(links.fold(gate).astype(BF), 0)
    down = links.send_y(links.fold(down).astype(BF), 1)

    mixed_grad = over_in(attn_grad_in, out_rows, True)
    heads_grad = attend_back(query, key, value, mixed_grad, lse, tables)
    heads_grad, up = tied(heads_grad, up)
    normed_grad = over_out([heads_grad], [heads_full], True)
    last = line_out(normed_grad)
    grad_heads = links.scatter_core(features, after(heads_grad, normed_grad), 0)
    cut = 2 * head_cols
    heads = links.send_y(grad_heads[:, :cut], 0)
    tail = links.send_x_first(grad_heads[:, cut:], 0)
    up = links.send_x(links.fold(after(up, grad_heads)).astype(BF), 0)
    grad_out = links.scatter_core(attended, after(attn_grad_in, grad_heads), 1)
    out = links.send_y(after(grad_out, heads), 1)
    grad_heads = links.fold(links.send_x(links.fold(heads).astype(BF), 0))
    tail = links.fold(links.send_y(links.fold(tail).astype(BF), 0))
    input_grad = rows_call(
        leave_body, (places,), (inputs[0], residual_grad, last), (high,)
    )[0]
    return (
        result[None],
        loss_value,
        input_grad[None],
        grad_heads[:, :head_cols],
        grad_heads[:, head_cols:],
        tail,
        links.fold(links.send_x(links.fold(out).astype(BF), 1)),
        links.fold(gate),
        links.fold(up),
        links.fold(down),
    )


def solution(mesh):
    if mesh.shape["dp"] == 8 and mesh.shape["tensor"] == 4:
        links = BlockLinks()
        mesh = Mesh(mesh.devices.reshape(2, 2, 2, 4), ("y", "x", "core", "z"))
    else:
        links = PlainLinks()
    dp, tensor = links.rows, links.line
    tokens = P(dp, tensor, None)
    rows = P(dp, tensor)
    cols = P(tensor, dp)
    in_specs = (tokens, tokens, P(dp), rows, rows, rows, cols, rows, rows, cols)
    out_specs = (tokens, P(), tokens, rows, rows, rows, cols, rows, rows, cols)

    def local(*args):
        return layer(links, *args)

    return jax.shard_map(
        local, mesh=mesh, in_specs=in_specs, out_specs=out_specs, check_vma=False
    )
```

```python
import functools
import math

import jax
import jax.numpy as jnp
from jax import lax
from jax.experimental import pallas as pl
from jax.experimental.pallas import tpu as pltpu
from jax.sharding import Mesh
from jax.sharding import PartitionSpec as P

HS = 128
EPSILON = 1e-05
BF = jnp.bfloat16
F32 = jnp.float32
NEGATIVE = -1e30


def statistics(values):
    centre = values - jnp.mean(values, axis=-1, keepdims=True)
    spread = jnp.mean(centre * centre, axis=-1, keepdims=True)
    inverse = lax.rsqrt(spread + EPSILON)
    return centre * inverse, inverse


def norm_back(values, grad_in):
    normed, inverse = statistics(values)
    return inverse * (
        grad_in
        - jnp.mean(grad_in, axis=-1, keepdims=True)
        - normed * jnp.mean(grad_in * normed, axis=-1, keepdims=True)
    )


def rotary_tables(length, size):
    half_size = size // 2
    inverse = jnp.exp(jnp.arange(half_size, dtype=F32) * (-2.0 * math.log(10000.0) / size))
    angles = jnp.arange(length, dtype=F32)[:, None] * inverse[None, :]
    cosine, sine = jnp.cos(angles), jnp.sin(angles)
    return (
        jnp.concatenate([cosine, cosine], axis=1),
        jnp.concatenate([-sine, sine], axis=1),
    )


def dot(left, right):
    return jnp.dot(left, right, preferred_element_type=F32)


def dot_nt(left, right):
    return lax.dot_general(left, right, (((1,), (1,)), ((), ())), preferred_element_type=F32)


def dot_tn(left, right):
    return lax.dot_general(left, right, (((0,), (0,)), ((), ())), preferred_element_type=F32)


def kernel_call(body, grid, ins, outs, args, flops, scratch=(), limit=48):
    args = tuple(
        pltpu.with_memory_space_constraint(a, pltpu.HBM) if a.size > 1024 else a for a in args
    )
    moved = sum(a.size * a.dtype.itemsize for a in args)
    moved += sum(math.prod(shape.shape) * shape.dtype.itemsize for shape, _ in outs)
    return pl.pallas_call(
        body,
        grid=grid,
        in_specs=ins,
        out_specs=[spec for _, spec in outs],
        out_shape=[pltpu.HBM(shape.shape, shape.dtype) for shape, _ in outs],
        scratch_shapes=list(scratch),
        compiler_params=pltpu.CompilerParams(
            dimension_semantics=("arbitrary",) * len(grid), vmem_limit_bytes=limit << 20
        ),
        cost_estimate=pl.CostEstimate(flops=flops, transcendentals=0, bytes_accessed=moved),
    )(*args)


def whole(array):
    rank = len(array.shape)
    return pl.BlockSpec(array.shape, lambda *_: (0,) * rank, pipeline_mode=pl.Buffered(1))


def shape_of(shape, dtype):
    return jax.ShapeDtypeStruct(shape, dtype)


def dot_parts(left, parts, transposed=False):
    total, start = None, 0
    for part in parts:
        depth = part.shape[1 if transposed else 0]
        got = (dot_nt if transposed else dot)(left[:, start : start + depth], part)
        total = got if total is None else total + got
        start += depth
    return total


def in_order(from_ref, x_ref):
    count = from_ref.shape[0]
    width = x_ref.shape[1] // count
    parts = [x_ref[:, block_at(from_ref, slot, width)] for slot in range(count)]
    return jnp.concatenate(parts, axis=1).astype(F32)


def heads_body(head_cols, count, from_ref, x_ref, *refs):
    weights = refs[:count]
    c_ref, s_ref, f_ref, q_ref, k_ref, v_ref = refs[count:]
    rows = statistics(in_order(from_ref, x_ref))[0].astype(BF)
    f_ref[...] = rows
    cosine, sine = c_ref[...], s_ref[...]
    for part, out_ref in enumerate((q_ref, k_ref, v_ref)):
        cols = slice(part * head_cols, (part + 1) * head_cols)
        got = dot_parts(rows, [w_ref[:, cols] for w_ref in weights])
        if part == 2:
            out_ref[...] = got.astype(BF)
            continue
        for start in range(0, head_cols, HS):
            head = got[:, start : start + HS]
            turned = head * cosine + pltpu.roll(head, HS // 2, axis=1) * sine
            if part == 0:
                turned = turned * (HS**-0.5)
            out_ref[:, start : start + HS] = turned.astype(BF)


def project_heads(places, states, weights, tables):
    tokens, width = states.shape
    head_cols = weights[0].shape[1] // 3
    rows = min(256, tokens)
    row_spec = pl.BlockSpec((rows, width), lambda i: (i, 0))
    table_spec = pl.BlockSpec((rows, HS), lambda i: (i, 0))
    out_spec = pl.BlockSpec((rows, head_cols), lambda i: (i, 0))
    out = (shape_of((tokens, head_cols), BF), out_spec)
    return kernel_call(
        functools.partial(heads_body, head_cols, len(weights)),
        (tokens // rows,),
        [pl.BlockSpec(memory_space=pltpu.SMEM), row_spec]
        + [*map(whole, weights), table_spec, table_spec],
        [(shape_of((tokens, width), BF), row_spec), out, out, out],
        (places, states, *weights, *tables),
        2 * tokens * width * 3 * head_cols,
    )


def residual_body(count, from_ref, x_ref, o_ref, *refs):
    weights = refs[:count]
    r_ref, b_ref = refs[count:]
    depth = o_ref.shape[2]
    total = []
    for w_ref in weights:
        part = None
        for z in range(o_ref.shape[0]):
            got = dot(o_ref[z], w_ref[z * depth : (z + 1) * depth, :])
            part = got if part is None else part + got
        total.append(part)
    total = in_order(from_ref, x_ref) + jnp.concatenate(total, axis=1)
    r_ref[...] = total
    b_ref[...] = statistics(total)[0].astype(BF)


def residual_rows(places, states, attended, weights):
    tokens, width = states.shape
    rows = min(256, tokens)
    row_spec = pl.BlockSpec((rows, width), lambda i: (i, 0))
    line, _, cols = attended.shape
    return kernel_call(
        functools.partial(residual_body, len(weights)),
        (tokens // rows,),
        [pl.BlockSpec(memory_space=pltpu.SMEM), row_spec]
        + [pl.BlockSpec((line, rows, cols), lambda i: (0, i, 0)), *map(whole, weights)],
        [(shape_of((tokens, width), F32), row_spec), (shape_of((tokens, width), BF), row_spec)],
        (places, states, attended, *weights),
        2 * tokens * width * line * cols,
    )


def causal_scores(query, keys, start):
    scores = dot_nt(query, keys)
    row = start + lax.broadcasted_iota(jnp.int32, scores.shape, 0)
    return jnp.where(row >= lax.broadcasted_iota(jnp.int32, scores.shape, 1), scores, NEGATIVE)


def attend_body(rows, q_ref, k_ref, v_ref, o_ref, lse_ref):
    for start in range(0, q_ref.shape[0], rows):
        end = start + rows
        scores = causal_scores(q_ref[start:end, :], k_ref[:end, :], start)
        largest = jnp.max(scores, axis=-1, keepdims=True)
        shifted = jnp.exp(scores - largest)
        total = jnp.sum(shifted, axis=-1, keepdims=True)
        share = (shifted * (1.0 / total)).astype(BF)
        o_ref[start:end, :] = dot(share, v_ref[:end, :]).astype(BF)
        lse_ref[start:end, :] = jnp.broadcast_to(largest + jnp.log(total), (rows, HS))


def attend(query, key, value):
    tokens, head_cols = query.shape
    spec = pl.BlockSpec((tokens, HS), lambda h: (0, h))
    return kernel_call(
        functools.partial(attend_body, min(256, tokens)),
        (head_cols // HS,),
        [spec] * 3,
        [(shape_of((tokens, head_cols), BF), spec), (shape_of((tokens, head_cols), F32), spec)],
        (query, key, value),
        3 * tokens * tokens * head_cols,
    )


def attend_back_body(
    rows, heads, q_ref, k_ref, v_ref, g_ref, lse_ref, c_ref, s_ref, out_ref, dk_ref, dv_ref
):
    tokens = q_ref.shape[0]
    place = pl.program_id(0) * HS
    dk_ref[...] = jnp.zeros_like(dk_ref)
    dv_ref[...] = jnp.zeros_like(dv_ref)

    def turn_back(values, start, end):
        return values * c_ref[start:end, :] - pltpu.roll(values, HS // 2, axis=1) * s_ref[
            start:end, :
        ]

    for start in range(0, tokens, rows):
        end = start + rows
        query, grad = q_ref[start:end, :], g_ref[start:end, :]
        keys, values = k_ref[:end, :], v_ref[:end, :]
        share = jnp.exp(causal_scores(query, keys, start) - lse_ref[start:end, :1])
        share_grad = dot_nt(grad, values)
        mean = jnp.sum(share_grad * share, axis=-1, keepdims=True)
        score_grad = (share * (share_grad - mean)).astype(BF)
        dv_ref[:end, :] += dot_tn(share.astype(BF), grad)
        dk_ref[:end, :] += dot_tn(score_grad, query)
        query_grad = turn_back(dot(score_grad, keys), start, end) * (HS**-0.5)
        out_ref[start:end, pl.ds(pl.multiple_of(place, HS), HS)] = query_grad.astype(BF)
    place_k = pl.multiple_of(place + heads * HS, HS)
    place_v = pl.multiple_of(place + 2 * heads * HS, HS)
    out_ref[:, pl.ds(place_k, HS)] = turn_back(dk_ref[...], 0, tokens).astype(BF)
    out_ref[:, pl.ds(place_v, HS)] = dv_ref[...].astype(BF)


def attend_back(query, key, value, grad, lse, tables):
    tokens, head_cols = query.shape
    heads = head_cols // HS
    spec = pl.BlockSpec((tokens, HS), lambda h: (0, h))
    out = shape_of((tokens, 3 * head_cols), BF)
    return kernel_call(
        functools.partial(attend_back_body, min(256, tokens), heads),
        (heads,),
        [spec] * 5 + [whole(tables[0]), whole(tables[1])],
        [(out, pl.BlockSpec(out.shape, lambda h: (0, 0)))],
        (query, key, value, grad, lse, *tables),
        6 * tokens * tokens * head_cols,
        scratch=[pltpu.VMEM((tokens, HS), F32)] * 2,
    )[0]


def column_blocks(array, size):
    return pl.BlockSpec((array.shape[0], size), lambda j: (0, j))


def row_blocks(array, size):
    return pl.BlockSpec((size, array.shape[1]), lambda j: (j, 0))


def gate_body(rows, count, x_ref, *refs):
    gates, ups = refs[:count], refs[count : 2 * count]
    hid_ref, gate_ref, up_ref = refs[2 * count :]
    for start in range(0, x_ref.shape[0], rows):
        part = slice(start, start + rows)
        gate = dot_parts(x_ref[part, :], [ref[...] for ref in gates])
        up = dot_parts(x_ref[part, :], [ref[...] for ref in ups])
        hid_ref[part, :] = (gate / (1.0 + jnp.exp(-gate)) * up).astype(BF)
        gate_ref[part, :] = gate.astype(BF)
        up_ref[part, :] = up.astype(BF)


def gate_up(tokens, gates, ups):
    count, size = gates[0].shape[1], 256
    shape = shape_of((tokens.shape[0], count), BF)
    out = (shape, column_blocks(shape, size))
    return kernel_call(
        functools.partial(gate_body, min(256, tokens.shape[0]), len(gates)),
        (count // size,),
        [whole(tokens)] + [column_blocks(part, size) for part in (*gates, *ups)],
        [out, out, out],
        (tokens, *gates, *ups),
        4 * tokens.size * count,
    )


def over_in_body(transposed, left_ref, *refs):
    refs[-1][...] = dot_parts(left_ref[...], [ref[...] for ref in refs[:-1]], transposed).astype(BF)


def over_in(left, parts, transposed):
    size = 256
    blocks = row_blocks if transposed else column_blocks
    count = parts[0].shape[0 if transposed else 1]
    shape = shape_of((left.shape[0], count), BF)
    return kernel_call(
        functools.partial(over_in_body, transposed),
        (count // size,),
        [whole(left)] + [blocks(part, size) for part in parts],
        [(shape, column_blocks(shape, size))],
        (left, *parts),
        2 * left.size * count,
    )[0]


def over_out_body(transposed, lefts, steps, *refs):
    parts = (len(refs) - 1 - lefts) // lefts
    for part in range(parts):

        @pl.when(pl.program_id(0) // steps == part)
        def _():
            total = None
            for i in range(lefts):
                right = refs[lefts + i * parts + part][...]
                got = (dot_nt if transposed else dot)(refs[i][...], right)
                total = got if total is None else total + got
            refs[-1][...] = total.astype(BF)


def over_out(lefts, rights, transposed):
    size = 512 if len(lefts) == 1 else 256
    free = 0 if transposed else 1
    steps = rights[0][0].shape[free] // size
    count = steps * len(rights[0])
    specs = []
    for parts in rights:
        for i, part in enumerate(parts):
            block = (size, part.shape[1]) if transposed else (part.shape[0], size)

            def place(j, i=i):
                at = jnp.clip(j - i * steps, 0, steps - 1)
                return (at, 0) if transposed else (0, at)

            specs.append(pl.BlockSpec(block, place))
    shape = shape_of((lefts[0].shape[0], count * size), BF)
    return kernel_call(
        functools.partial(over_out_body, transposed, len(lefts), steps),
        (count,),
        [whole(left) for left in lefts] + specs,
        [(shape, column_blocks(shape, size))],
        (*lefts, *(part for parts in rights for part in parts)),
        sum(2 * left.size for left in lefts) * count * size,
    )[0]


def hidden_back_body(rows, count, y_ref, *refs):
    gate_ref, up_ref, dg_ref, du_ref = refs[count:]
    for start in range(0, y_ref.shape[0], rows):
        part = slice(start, start + rows)
        grad = dot_parts(y_ref[part, :], [ref[...] for ref in refs[:count]], True)
        gate, up = gate_ref[part, :].astype(F32), up_ref[part, :].astype(F32)
        sigmoid = 1.0 / (1.0 + jnp.exp(-gate))
        dg_ref[part, :] = (grad * up * sigmoid * (1.0 + gate * (1.0 - sigmoid))).astype(BF)
        du_ref[part, :] = (grad * (gate * sigmoid)).astype(BF)


def hidden_back(grad, downs, gate, up):
    count, size = downs[0].shape[0], 256
    shape = shape_of((grad.shape[0], count), BF)
    out = (shape, column_blocks(shape, size))
    return kernel_call(
        functools.partial(hidden_back_body, min(256, grad.shape[0]), len(downs)),
        (count // size,),
        [whole(grad)]
        + [row_blocks(part, size) for part in downs]
        + [column_blocks(gate, size), column_blocks(up, size)],
        [out, out],
        (grad, *downs, gate, up),
        2 * grad.size * count,
    )


ROWS = 64


def rows_call(body, scalars, arrays, outs):
    rows, width = arrays[0].shape
    size = min(ROWS, rows)
    spec = pl.BlockSpec((size, width), lambda i: (i, 0))
    out = []
    for shape, dtype in outs:
        block = (8, 128) if shape[1] == 128 else (size, width)
        out.append((shape_of(shape, dtype), pl.BlockSpec(block, lambda i: (i, 0))))
    return kernel_call(
        body,
        (rows // size,),
        [pl.BlockSpec(memory_space=pltpu.SMEM)] * len(scalars) + [spec] * len(arrays),
        out,
        (*scalars, *arrays),
        10 * rows * width,
        limit=32,
    )


def block_at(from_ref, slot, width):
    return pl.ds(pl.multiple_of(from_ref[slot] * width, 128), width)


def loss_body(
    from_ref, length_ref, scale_ref, r_ref, part_ref, t_ref, out_ref, grad_ref, low_ref, sq_ref
):
    count = from_ref.shape[0]
    width = t_ref.shape[1] // count
    size = r_ref.shape[0]
    row = pl.program_id(0) * size + lax.broadcasted_iota(jnp.int32, (size, width), 0)
    valid = row < length_ref[0]
    squares = jnp.zeros((size, width), F32)
    for slot in range(count):
        here = slice(slot * width, (slot + 1) * width)
        there = block_at(from_ref, slot, width)
        result = r_ref[:, here] + part_ref[:, here].astype(F32)
        out_ref[:, there] = result.astype(BF)
        error = jnp.where(valid, result - t_ref[:, there].astype(F32), 0.0)
        squares += error * error
        grad = error * scale_ref[0]
        grad_ref[:, here] = grad
        low_ref[:, here] = grad.astype(BF)
    sq_ref[...] = jnp.full(sq_ref.shape, jnp.sum(squares), F32)


def middle_back_body(grad_ref, r_ref, part_ref, out_ref, low_ref):
    total = grad_ref[...] + norm_back(r_ref[...], part_ref[...].astype(F32))
    out_ref[...] = total
    low_ref[...] = total.astype(BF)


def leave_body(from_ref, x_ref, grad_ref, part_ref, out_ref):
    count = from_ref.shape[0]
    width = x_ref.shape[1] // count
    total = grad_ref[...] + norm_back(in_order(from_ref, x_ref), part_ref[...].astype(F32))
    for slot in range(count):
        out_ref[:, block_at(from_ref, slot, width)] = total[:, slot * width : (slot + 1) * width]


class PlainLinks:
    line = "tensor"
    rows = "dp"

    def sources(self):
        return jnp.zeros((1,), jnp.int32)

    def gather_x(self, shard, axis, late=()):
        return lax.all_gather(shard, "dp", axis=axis, tiled=True)

    def gather_y(self, value, axis, late=()):
        return value

    def begin_y(self, value):
        return (value,)

    def end(self, pair, axis):
        return pair[0]

    def gather_y_first(self, shard, axis):
        return shard

    def gather_x_last(self, value, axis, late=()):
        return lax.all_gather(value, "dp", axis=axis, tiled=True)

    def gather_core(self, value):
        return (value,)

    def scatter_core(self, left, right, axis):
        grad = dot_tn(left, right).astype(BF)
        return lax.psum_scatter(grad, "dp", scatter_dimension=axis, tiled=True)

    def send_y(self, grad, axis):
        return (grad,)

    def send_x(self, grad, axis):
        return (grad,)

    def send_x_first(self, grad, axis):
        return (grad,)

    def fold(self, sent):
        return sent[0].astype(F32)

    def total(self, value, everywhere):
        return lax.psum(value, ("dp", "tensor") if everywhere else "dp")


SWAP = [(0, 1), (1, 0)]


def halves(values, axis):
    size = values.shape[axis] // 2
    return (
        lax.slice_in_dim(values, 0, size, axis=axis),
        lax.slice_in_dim(values, size, 2 * size, axis=axis),
    )


class BlockLinks:
    line = "z"
    rows = ("y", "x", "core")

    def swap(self, values, axis):
        return lax.ppermute(values, axis, SWAP)

    def sources(self):
        slot = jnp.arange(8, dtype=jnp.int32)
        y, core = lax.axis_index("y"), lax.axis_index("core")
        return (y ^ (slot // 2 % 2)) * 4 + slot % 2 * 2 + (core ^ (slot // 4))

    def of_x(self, values, axis, flip=False):
        size = values.shape[axis] // 2
        place = lax.axis_index("x")
        if flip:
            place = 1 - place
        return lax.dynamic_slice_in_dim(values, place * size, size, axis=axis)

    def gather_x(self, shard, axis, late=()):
        other = after(self.swap(shard, "x"), *late)
        first = lax.axis_index("x") == 0
        return jnp.concatenate(
            [jnp.where(first, shard, other), jnp.where(first, other, shard)], axis=axis
        )

    def gather_y(self, value, axis, late=()):
        return jnp.concatenate([value, after(self.swap(value, "y"), *late)], axis=axis)

    def begin_y(self, value):
        return (value, self.swap(value, "y"))

    def end(self, pair, axis):
        return jnp.concatenate(pair, axis=axis)

    def gather_y_first(self, shard, axis):
        return jnp.concatenate([shard, self.swap(shard, "y")], axis=axis)

    def gather_x_last(self, value, axis, late=()):
        other = after(self.swap(value, "x"), *late)
        first = lax.axis_index("x") == 0
        parts = []
        for own, far in zip(halves(value, axis), halves(other, axis)):
            parts += [jnp.where(first, own, far), jnp.where(first, far, own)]
        return jnp.concatenate(parts, axis=axis)

    def gather_core(self, value):
        return (value, self.swap(value, "core"))

    def scatter_core(self, left, right, axis):
        if axis == 0:
            keep, send = halves(left, 1)
            received = self.swap(dot_tn(send, right).astype(BF), "core")
            return (dot_tn(keep, right) + received.astype(F32)).astype(BF)
        keep, send = halves(right, 1)
        received = self.swap(dot_tn(left, send).astype(BF), "core")
        return (dot_tn(left, keep) + received.astype(F32)).astype(BF)

    def send_y(self, grad, axis):
        keep, send = halves(grad, axis)
        return (keep, self.swap(send, "y"))

    def send_x(self, grad, axis):
        return (self.of_x(grad, axis), self.swap(self.of_x(grad, axis, flip=True), "x"))

    def send_x_first(self, grad, axis):
        pairs = halves(grad, axis)
        send = jnp.concatenate([self.of_x(pair, axis, flip=True) for pair in pairs], axis=axis)
        keep = jnp.concatenate([self.of_x(pair, axis) for pair in pairs], axis=axis)
        return (keep, self.swap(send, "x"))

    def fold(self, sent):
        return sent[0].astype(F32) + sent[1].astype(F32)

    def total(self, value, everywhere):
        value = jnp.full((8, 128), value, F32)
        for name in self.rows:
            value = value + self.swap(value, name)
        for step in (1, 2) if everywhere else ():
            value = value + lax.ppermute(value, "z", [(i, i ^ step) for i in range(4)])
        return value[0, 0]


def tied(*values):
    return lax.optimization_barrier(values)


def after(value, *others):
    return lax.optimization_barrier((value, others))[0]


def layer(links, inputs, teacher, lengths, w_query, w_key, w_value, w_out, w_gate, w_up, w_down):
    line = links.line
    local_rows = inputs.shape[1]
    slot_count = local_rows * lax.axis_size(line)
    token_total = slot_count * lax.axis_size(links.rows)
    width_all = inputs.shape[2]
    head_cols = w_query.shape[1]

    def line_in(values):
        return lax.all_gather(values, line, axis=0, tiled=True)

    def line_out(partial):
        return lax.psum_scatter(partial, line, scatter_dimension=0, tiled=True)

    shape = inputs.shape[1:]
    low, high = (shape, BF), (shape, F32)
    places = links.sources()
    own_length = lengths[0]
    valid_total = links.total(own_length.astype(F32), False)
    scale = (token_total / valid_total).reshape(1)
    left_length = (own_length - lax.axis_index(line) * local_rows).reshape(1)
    tables = rotary_tables(slot_count, HS)
    states = line_in(inputs[0])

    heads_full = links.gather_x(jnp.concatenate([w_query, w_key, w_value], axis=1), 0)
    heads_full = links.gather_y(heads_full, 0)
    gate_full = links.gather_x(w_gate, 0)
    down_full = links.gather_x(after(w_down, gate_full), 1)
    heads_full, gate_full = tied(heads_full, gate_full)
    heads_full = links.gather_core(heads_full)
    up_full = links.gather_y_first(w_up, 0)
    states, tables, scale, down_full, up_full = tied(states, tables, scale, down_full, up_full)
    out_full = lax.all_gather(after(w_out, states), line, axis=0, tiled=True)
    features, query, key, value = project_heads(places, states, heads_full, tables)
    gate_full = links.begin_y(gate_full)
    up_full = links.gather_x_last(up_full, 0, (query,))

    attended, lse = attend(query, key, value)
    attended, up_full, gate_full = tied(attended, up_full, gate_full)
    out_full = links.gather_y_first(after(out_full, attended), 1)
    out_full = links.gather_x_last(out_full, 1)
    down_full = links.gather_y(down_full, 1)
    gate_full = links.end(after(gate_full, attended), 0)
    everyone = lax.all_gather(attended, line, axis=0)
    everyone, out_full, down_full = tied(everyone, out_full, down_full)
    out_full = links.gather_core(out_full)
    gate_full = links.gather_core(gate_full)
    up_full = links.gather_core(up_full)
    residual, features_two = residual_rows(places, states, everyone, out_full)
    down_full = links.gather_core(after(down_full, features_two))
    place = lax.axis_index(line)
    residual = lax.dynamic_slice_in_dim(residual, place * local_rows, local_rows, axis=0)
    out_rows = tuple(
        lax.dynamic_slice_in_dim(part, place * head_cols, head_cols, axis=0) for part in out_full
    )
    hidden, gate_pre, up_pre = gate_up(features_two, gate_full, up_full)
    mlp_out = line_out(over_out([hidden], [down_full], False))
    result, grad_result, grad_low, squares = rows_call(
        loss_body,
        (places, left_length, scale),
        (residual, mlp_out, teacher[0]),
        (low, high, low, ((local_rows // ROWS * 8, 128), F32)),
    )
    total_squares = links.total(jnp.sum(squares[::8, 0]), True)
    loss_value = total_squares / (valid_total * width_all)

    down_grad_in = line_in(grad_low)
    down_grad_in, loss_value = tied(down_grad_in, loss_value)
    gate_grad, up_grad = hidden_back(down_grad_in, down_full, gate_pre, up_pre)
    partial = over_out([gate_grad, up_grad], [gate_full, up_full], True)
    middle_grad = line_out(partial)
    features_two, hidden = after((features_two, hidden), partial)
    gate = links.scatter_core(features_two, gate_grad, 0)
    down = links.scatter_core(hidden, down_grad_in, 1)
    up = links.scatter_core(features_two, up_grad, 0)
    middle_grad, gate, down, up = tied(middle_grad, gate, down, up)
    gate = links.send_y(gate, 0)
    down = links.send_x_first(down, 1)
    up = links.send_y(up, 0)
    residual_grad, residual_low = rows_call(
        middle_back_body, (), (grad_result, residual, middle_grad), (high, low)
    )
    attn_grad_in = line_in(residual_low)
    attn_grad_in, gate, down = tied(attn_grad_in, gate, down)
    gate = links.send_x(links.fold(gate).astype(BF), 0)
    down = links.send_y(links.fold(down).astype(BF), 1)

    mixed_grad = over_in(attn_grad_in, out_rows, True)
    heads_grad = attend_back(query, key, value, mixed_grad, lse, tables)
    heads_grad, up = tied(heads_grad, up)
    normed_grad = over_out([heads_grad], [heads_full], True)
    last = line_out(normed_grad)
    grad_heads = links.scatter_core(features, after(heads_grad, normed_grad), 0)
    cut = 2 * head_cols
    heads = links.send_y(grad_heads[:, :cut], 0)
    tail = links.send_x_first(grad_heads[:, cut:], 0)
    up = links.send_x(links.fold(after(up, grad_heads)).astype(BF), 0)
    grad_out = links.scatter_core(attended, after(attn_grad_in, grad_heads), 1)
    out = links.send_y(after(grad_out, heads), 1)
    grad_heads = links.fold(links.send_x(links.fold(heads).astype(BF), 0))
    tail = links.fold(links.send_y(links.fold(tail).astype(BF), 0))
    input_grad = rows_call(
        leave_body, (places,), (inputs[0], residual_grad, last), (high,)
    )[0]
    return (
        result[None],
        loss_value,
        input_grad[None],
        grad_heads[:, :head_cols],
        grad_heads[:, head_cols:],
        tail,
        links.fold(links.send_x(links.fold(out).astype(BF), 1)),
        links.fold(gate),
        links.fold(up),
        links.fold(down),
    )


def solution(mesh):
    if mesh.shape["dp"] == 8 and mesh.shape["tensor"] == 4:
        links = BlockLinks()
        mesh = Mesh(mesh.devices.reshape(2, 2, 2, 4), ("y", "x", "core", "z"))
    else:
        links = PlainLinks()
    dp, tensor = links.rows, links.line
    tokens = P(dp, tensor, None)
    rows = P(dp, tensor)
    cols = P(tensor, dp)
    in_specs = (tokens, tokens, P(dp), rows, rows, rows, cols, rows, rows, cols)
    out_specs = (tokens, P(), tokens, rows, rows, rows, cols, rows, rows, cols)

    def local(*args):
        return layer(links, *args)

    return jax.shard_map(
        local, mesh=mesh, in_specs=in_specs, out_specs=out_specs, check_vma=False
    )
```
